512 devices in a mesh: ctx: 64 (over z, y_hi, core), head: 8 (over x, y_lo).
Axes of the slice: x: 4, y: 8 (y_hi: 4, y_lo: 2; y = y_hi * 2 + y_lo), z: 8, core: 2. Of those that a mesh axis runs over, the one named last changes fastest.
Arguments:
- queries: bfloat16 [65536, 4096], P('ctx', 'head'), may hold values from -10 to 10, as said below
- keys: bfloat16 [65536, 4096], P('ctx', 'head'), may hold values from -4.6 to 4.6, as said below
- values: bfloat16 [65536, 4096], P('ctx', 'head'), may hold values from -6 to 6
Outputs:
- attended: bfloat16 [65536, 4096], P('ctx', 'head')
The draws below stay inside these ranges and needn't reach their ends.
Inputs may be any that keep to these rules, and one draw needn't show every extreme that they name: real-valued queries. real-valued keys.
All inputs are finite; a program needn't handle non-finite values.
Results may differ from the reference program's by a relative error of at most 0.0099.
Values may be sent and summed in bfloat16 or wider, within the bound.
No kernel may reach another device: no remote copies, remote signals or barrier semaphores. Data moves between devices by JAX's collectives and lax.ppermute only.
A program may use at most 64 MiB of HBM per device.

```python
import jax
import jax.numpy as jnp
from jax import lax

HEADS = 32
HD = 128
TOK_DEV = 1024
POOL = 256
EDGE = 256
SEQ = 65536
LEVELS = 6
N_CTX = 64


def draw_queries(key, part):
    noise_key = jax.random.fold_in(key, 1)
    base = jnp.clip(2.5 * jax.random.normal(noise_key, (SEQ, HEADS * HD), jnp.float32), -10.0, 10.0)
    return base.astype(jnp.bfloat16)


def draw_keys(key, part):
    noise_key = jax.random.fold_in(key, 2)
    base = jnp.clip(jax.random.normal(noise_key, (SEQ, HEADS * HD), jnp.float32), -4.0, 4.0)
    return base.astype(jnp.bfloat16)


def level_of(rng, extent, cuts, least, high):
    def one(position, shards_of):
        steps = jax.random.uniform(jax.random.fold_in(jax.random.fold_in(rng, 6), position), (shards_of,), jnp.float32, least / len(cuts), high / len(cuts))
        return jnp.repeat(jnp.exp(steps), extent[position] // shards_of).reshape((-1,) + (1,) * (len(extent) - position - 1))

    loudness = one(*cuts[0])
    for cut in cuts[1:]:
        loudness = loudness * one(*cut)
    return loudness


def noise(rng, dims, scale, bound, shards=(), held_as=jnp.bfloat16):
    values = scale * jax.random.normal(rng, dims, jnp.float32)
    if shards:
        values = values * level_of(rng, dims, shards, -0.22, 0.18)
    return jnp.clip(values, -bound, bound).astype(held_as)


def setup_inputs(seed: int = 0) -> dict:
    streams_of = jax.random.split(jax.random.key(seed), 4)
    queries = draw_queries(jax.random.fold_in(streams_of[3], 71), 0)
    keys = draw_keys(jax.random.fold_in(streams_of[3], 71), 0)
    values = noise(streams_of[2], (SEQ, HEADS * HD), 1.0, 6.0, ((0, 64), (1, 8)))
    return dict(queries=queries, keys=keys, values=values)


def pool_rows(block, group):
    shape = block.shape
    grouped = block.reshape(shape[:-2] + (shape[-2] // group, group, shape[-1])).astype(jnp.float32)
    return (jnp.sum(grouped, axis=-2) / jnp.float32(group ** 0.5)).astype(jnp.bfloat16)


def reference(queries, keys, values):
    width = HEADS * HD
    scale = jnp.float32(HD ** -0.5)
    query_blocks = queries.reshape(N_CTX, TOK_DEV, width)
    paired = jnp.stack((keys.reshape(N_CTX, TOK_DEV, width), values.reshape(N_CTX, TOK_DEV, width)))
    summaries = []
    level = pool_rows(paired, TOK_DEV // POOL)
    for depth in range(LEVELS):
        summaries.append(level)
        if depth + 1 < LEVELS:
            merged = level.reshape(2, N_CTX // (2 ** (depth + 1)), 2 * POOL, width)
            level = pool_rows(merged, 2)
    blank = jnp.zeros((2, 1, TOK_DEV, width), jnp.bfloat16)
    padded = jnp.concatenate([blank, paired, blank], axis=1)

    def one_block(index):
        own = lax.dynamic_index_in_dim(paired, index, 1, keepdims=False)
        left = lax.dynamic_index_in_dim(padded, index, 1, keepdims=False)[:, TOK_DEV - EDGE:]
        right = lax.dynamic_index_in_dim(padded, index + 2, 1, keepdims=False)[:, :EDGE]
        pieces = [own, left, right]
        for depth in range(LEVELS):
            sibling = jnp.bitwise_xor(index // (2 ** depth), 1).astype(jnp.int32)
            pieces.append(lax.dynamic_index_in_dim(summaries[depth], sibling, 1, keepdims=False))
        key_set = jnp.concatenate(pieces, axis=1)
        total = key_set.shape[1]
        valid = jnp.concatenate([
            jnp.ones((TOK_DEV,), bool),
            jnp.broadcast_to(index > 0, (EDGE,)),
            jnp.broadcast_to(index < N_CTX - 1, (EDGE,)),
            jnp.ones((total - TOK_DEV - 2 * EDGE,), bool)])
        query = lax.dynamic_index_in_dim(query_blocks, index, 0, keepdims=False)
        query = query.astype(jnp.float32).reshape(TOK_DEV, HEADS, HD)
        key_all = key_set[0].astype(jnp.float32).reshape(total, HEADS, HD)
        value_all = key_set[1].astype(jnp.float32).reshape(total, HEADS, HD)
        scores = jnp.einsum('qhd,khd->hqk', query, key_all) * scale
        scores = jnp.where(valid[None, None, :], scores, jnp.float32(-1e30))
        peak = jnp.max(scores, axis=-1, keepdims=True)
        probs = jnp.exp(scores - peak)
        denom = jnp.sum(probs, axis=-1)
        weights = probs.astype(jnp.bfloat16)
        numer = jnp.einsum('hqk,khd->qhd', weights.astype(jnp.float32), value_all)
        result = numer / jnp.transpose(denom)[:, :, None]
        return result.astype(jnp.bfloat16).reshape(TOK_DEV, width)

    outputs = lax.map(one_block, jnp.arange(N_CTX, dtype=jnp.int32))
    return outputs.reshape(SEQ, width)
```

```python
import functools

import jax
import jax.numpy as jnp
from jax import lax
from jax.experimental import pallas as pl
from jax.experimental.pallas import tpu as pltpu
from jax.sharding import PartitionSpec as P


HD = 128
HEADS_DEV = 4
WIDTH = HEADS_DEV * HD
TOK = 1024
POOL = 256
EDGE = 256
N_CTX = 64
SCALE_LOG2 = (HD**-0.5) * 1.4426950408889634
Q_TILE = 256


def swap(value, partner):
    pairs = []
    for source in range(N_CTX):
        z, y, core = source // 8, (source // 2) % 4, source % 2
        target = partner(z, y, core)
        if target is not None:
            pairs.append((source, target))
    return lax.ppermute(value, "ctx", pairs)


def index_of(z, y, core):
    return (z * 4 + y) * 2 + core


def other_core(z, y, core):
    return index_of(z, y, 1 - core)


def along_y(bits):
    return lambda z, y, core: index_of(z, y ^ bits, core)


def along_z(bits):
    return lambda z, y, core: index_of(z ^ bits, y, core)


def beside(z, y, core):
    here = index_of(z, y, core)
    there = here + 1 if core else here - 1
    return there if 0 <= there < N_CTX else None


def pooling_matrix(rows, group):
    out = lax.broadcasted_iota(jnp.int32, (rows // group, rows), 0)
    src = lax.broadcasted_iota(jnp.int32, (rows // group, rows), 1)
    return (src // group == out).astype(jnp.float32).astype(jnp.bfloat16)


def pool(value, group, matrix):
    total = jnp.dot(matrix, value, preferred_element_type=jnp.float32)
    return (total / jnp.float32(group**0.5)).astype(jnp.bfloat16)


def first_kernel(core_ref, k_ref, v_ref, near_ref, far_ref, one_ref, two_ref):
    core = core_ref[0]
    by4 = pooling_matrix(256, 4)
    by2 = pooling_matrix(256, 2)
    for side, ref in enumerate((k_ref, v_ref)):
        cols = pl.ds(side * WIDTH, WIDTH)
        for part in range(4):
            near_ref[pl.ds(part * 64, 64), cols] = pool(ref[pl.ds(part * 256, 256), :], 4, by4)
        one = pool(near_ref[pl.ds(0, 256), cols], 2, by2)
        one_ref[:, cols] = one
        two_ref[:, cols] = pool(one, 2, by2[:64, :128])
        last = pl.multiple_of((1 - core) * (TOK - EDGE), EDGE)
        near_ref[pl.ds(POOL, EDGE), cols] = ref[pl.ds(last, EDGE), :]
        first = pl.multiple_of(core * (TOK - EDGE), EDGE)
        far_ref[:, cols] = ref[pl.ds(first, EDGE), :]


def first_pools(core, keys, values):
    shape = lambda rows: jax.ShapeDtypeStruct((rows, 2 * WIDTH), jnp.bfloat16)
    vmem = pl.BlockSpec(memory_space=pltpu.VMEM)
    return pl.pallas_call(
        first_kernel,
        in_specs=[pl.BlockSpec(memory_space=pltpu.SMEM), vmem, vmem],
        out_specs=[vmem] * 4,
        out_shape=[shape(512), shape(256), shape(128), shape(64)],
        cost_estimate=pl.CostEstimate(flops=10**8, bytes_accessed=4 * 2**20, transcendentals=0),
        name="first_pools",
    )(core, keys, values)


def plane_kernel(own_ref, a_ref, b_ref, c_ref, got_ref, three_ref, four_ref, five_ref):
    by2 = pooling_matrix(256, 2)
    a, b, c = a_ref[...], b_ref[...], c_ref[...]
    got_ref[pl.ds(0, 128), :] = a
    got_ref[pl.ds(128, 64), :] = b
    got_ref[pl.ds(192, 64), :] = c
    a = pool(a, 2, by2[:64, :128])
    rows = jnp.concatenate([own_ref[...], a, b, c], axis=0)
    three = pool(rows, 2, by2)
    four = pool(three, 2, by2[:64, :128])
    three_ref[...] = three
    four_ref[...] = four
    five_ref[...] = pool(four, 2, by2[:32, :64])


def plane_pools(own, a, b, c):
    shape = lambda rows: jax.ShapeDtypeStruct((rows, 2 * WIDTH), jnp.bfloat16)
    vmem = pl.BlockSpec(memory_space=pltpu.VMEM)
    return pl.pallas_call(
        plane_kernel,
        in_specs=[vmem] * 4,
        out_specs=[vmem] * 4,
        out_shape=[shape(256), shape(128), shape(64), shape(32)],
        cost_estimate=pl.CostEstimate(flops=10**8, bytes_accessed=2 * 2**20, transcendentals=0),
        name="plane_pools",
    )(own, a, b, c)


def attend_kernel(plan, carried, final, *refs):
    refs = list(refs)
    bias = refs.pop(0)[0]
    q_ref = refs.pop(0)
    pieces = []
    for masked in plan:
        pieces.append((refs.pop(0), refs.pop(0), masked))
    if carried:
        acc_in, m_in, l_in = refs.pop(0), refs.pop(0), refs.pop(0)
    for tile in range(TOK // Q_TILE):
        cols = pl.ds(tile * Q_TILE, Q_TILE)
        query = q_ref[cols, :]
        scores = []
        for k_ref, _, masked in pieces:
            s = lax.dot_general(
                k_ref[...], query, (((1,), (1,)), ((), ())), preferred_element_type=jnp.float32
            )
            scores.append(s + bias if masked else s)
        peak = functools.reduce(jnp.maximum, [jnp.max(s, axis=0, keepdims=True) for s in scores])
        if carried:
            before = m_in[0, :, cols]
            peak = jnp.maximum(peak, before)
            fade = jnp.exp2((before - peak) * SCALE_LOG2)
            total = l_in[0, :, cols] * fade
            acc = acc_in[0, :, cols] * fade
        else:
            total, acc = 0.0, 0.0
        for s, (_, v_ref, _) in zip(scores, pieces):
            p = jnp.exp2((s - peak) * SCALE_LOG2)
            total = total + jnp.sum(p, axis=0, keepdims=True)
            acc = acc + lax.dot_general(
                v_ref[...],
                p.astype(jnp.bfloat16),
                (((0,), (0,)), ((), ())),
                preferred_element_type=jnp.float32,
            )
        if final:
            refs[0][cols, :] = (acc / total).T.astype(jnp.bfloat16)
        else:
            refs[0][0, :, cols] = acc
            refs[1][0, :, cols] = peak
            refs[2][0, :, cols] = total


def attend(bias, queries, pieces, state, final):
    head = lambda rows, first: pl.BlockSpec((rows, HD), lambda h: (0, first + h))
    per_head = lambda rows: pl.BlockSpec((1, rows, TOK), lambda h: (h, 0, 0))
    in_specs = [pl.BlockSpec(memory_space=pltpu.SMEM), head(TOK, 0)]
    operands = [bias, queries]
    count = 0
    for k, v, first, _ in pieces:
        in_specs += [head(k.shape[0], 0), head(v.shape[0], first)]
        operands += [k, v]
        count += k.shape[0]
    if state is not None:
        in_specs += [per_head(HD), per_head(1), per_head(1)]
        operands += list(state)
    if final:
        out_specs = head(TOK, 0)
        out_shape = jax.ShapeDtypeStruct((TOK, WIDTH), jnp.bfloat16)
    else:
        out_specs = [per_head(HD), per_head(1), per_head(1)]
        out_shape = [
            jax.ShapeDtypeStruct((HEADS_DEV, rows, TOK), jnp.float32) for rows in (HD, 1, 1)
        ]
    return pl.pallas_call(
        functools.partial(attend_kernel, tuple(p[3] for p in pieces), state is not None, final),
        grid=(HEADS_DEV,),
        in_specs=in_specs,
        out_specs=out_specs,
        out_shape=out_shape,
        compiler_params=pltpu.CompilerParams(
            dimension_semantics=("arbitrary",), vmem_limit_bytes=48 * 2**20
        ),
        cost_estimate=pl.CostEstimate(
            flops=4 * TOK * count * WIDTH,
            bytes_accessed=2 * TOK * WIDTH + 4 * count * WIDTH + 4 * TOK * WIDTH,
            transcendentals=TOK * count * HEADS_DEV,
        ),
    )(*operands)


def on_device(queries, keys, values):
    position = lax.axis_index("ctx")
    core = (position % 2).astype(jnp.int32).reshape(1)
    outer = (position == 0) | (position == N_CTX - 1)
    bias = jnp.where(outer, jnp.float32(-1e30), jnp.float32(0)).reshape(1)

    near, far, one, two = first_pools(core, keys, values)
    got2 = swap(two, along_y(2))
    got1 = swap(one, along_y(1))
    got3 = swap(two, along_y(3))
    near_got = swap(near, other_core)
    state = attend(bias, queries, [(keys, values, 0, False)], None, False)
    planes, three, four, five = plane_pools(two, got1, got2, got3)
    from_z = [swap(five, along_z(b)) for b in (4, 5, 6, 7)]
    from_z += [swap(four, along_z(b)) for b in (2, 3)]
    from_z += [swap(three, along_z(1))]
    far_got = swap(far, beside)
    planes_got = swap(planes, other_core)
    pieces = [(x, x, HEADS_DEV, False) for x in (near_got, planes, planes_got)]
    pieces += [(far_got, far_got, HEADS_DEV, True)]
    state = attend(bias, queries, pieces, state, False)
    upper = jnp.concatenate(from_z, axis=0)
    upper_got = swap(upper, other_core)
    state = attend(bias, queries, [(upper, upper, HEADS_DEV, False)], state, False)
    return attend(bias, queries, [(upper_got, upper_got, HEADS_DEV, False)], state, True)


def solution(mesh):
    return jax.shard_map(
        on_device,
        mesh=mesh,
        in_specs=(P("ctx", "head"), P("ctx", "head"), P("ctx", "head")),
        out_specs=P("ctx", "head"),
        check_vma=False,
    )
```

```python
import functools

import jax
import jax.numpy as jnp
from jax import lax
from jax.experimental import pallas as pl
from jax.experimental.pallas import tpu as pltpu
from jax.sharding import PartitionSpec as P


HD = 128
HEADS_DEV = 4
WIDTH = HEADS_DEV * HD
TOK = 1024
POOL = 256
EDGE = 256
N_CTX = 64
SCALE_LOG2 = (HD**-0.5) * 1.4426950408889634
Q_TILE = 128
TOTAL_LIMIT = 2.0**100
VMEM_LIMIT = 24 * 2**20


def swap(value, partner):
    pairs = []
    for source in range(N_CTX):
        z, y, core = source // 8, (source // 2) % 4, source % 2
        target = partner(z, y, core)
        if target is not None:
            pairs.append((source, target))
    return lax.ppermute(value, "ctx", pairs)


def index_of(z, y, core):
    return (z * 4 + y) * 2 + core


def other_core(z, y, core):
    return index_of(z, y, 1 - core)


def along_y(bits):
    return lambda z, y, core: index_of(z, y ^ bits, core)


def along_z(bits):
    return lambda z, y, core: index_of(z ^ bits, y, core)


def beside(z, y, core):
    here = index_of(z, y, core)
    there = here + 1 if core else here - 1
    return there if 0 <= there < N_CTX else None


def pooling_matrix(rows, group):
    out = lax.broadcasted_iota(jnp.int32, (rows // group, rows), 0)
    src = lax.broadcasted_iota(jnp.int32, (rows // group, rows), 1)
    return (src // group == out).astype(jnp.float32).astype(jnp.bfloat16)


def pool(value, group, matrix):
    total = jnp.dot(matrix, value, preferred_element_type=jnp.float32)
    return (total / jnp.float32(group**0.5)).astype(jnp.bfloat16)


def first_kernel(core_ref, k_ref, v_ref, near_ref, far_ref, one_ref, two_ref):
    core = core_ref[0]
    by4 = pooling_matrix(256, 4)
    by2 = pooling_matrix(256, 2)
    for side, ref in enumerate((k_ref, v_ref)):
        cols = pl.ds(side * WIDTH, WIDTH)
        for part in range(4):
            near_ref[pl.ds(part * 64, 64), cols] = pool(ref[pl.ds(part * 256, 256), :], 4, by4)
        one = pool(near_ref[pl.ds(0, 256), cols], 2, by2)
        one_ref[:, cols] = one
        two_ref[:, cols] = pool(one, 2, by2[:64, :128])
        last = pl.multiple_of((1 - core) * (TOK - EDGE), EDGE)
        near_ref[pl.ds(POOL, EDGE), cols] = ref[pl.ds(last, EDGE), :]
        first = pl.multiple_of(core * (TOK - EDGE), EDGE)
        far_ref[:, cols] = ref[pl.ds(first, EDGE), :]


def first_pools(core, keys, values):
    shape = lambda rows: jax.ShapeDtypeStruct((rows, 2 * WIDTH), jnp.bfloat16)
    vmem = pl.BlockSpec(memory_space=pltpu.VMEM)
    return pl.pallas_call(
        first_kernel,
        in_specs=[pl.BlockSpec(memory_space=pltpu.SMEM), vmem, vmem],
        out_specs=[vmem] * 4,
        out_shape=[shape(512), shape(256), shape(128), shape(64)],
        compiler_params=pltpu.CompilerParams(vmem_limit_bytes=VMEM_LIMIT),
        cost_estimate=pl.CostEstimate(flops=10**8, bytes_accessed=4 * 2**20, transcendentals=0),
        name="first_pools",
    )(core, keys, values)


def small_call(kernel, rows, *operands):
    vmem = pl.BlockSpec(memory_space=pltpu.VMEM)
    return pl.pallas_call(
        kernel,
        in_specs=[vmem] * len(operands),
        out_specs=[vmem] * len(rows),
        out_shape=[jax.ShapeDtypeStruct((r, 2 * WIDTH), jnp.bfloat16) for r in rows],
        compiler_params=pltpu.CompilerParams(vmem_limit_bytes=VMEM_LIMIT),
        cost_estimate=pl.CostEstimate(flops=10**8, bytes_accessed=2**20, transcendentals=0),
    )(*operands)


def plane_kernel(own_ref, a_ref, b_ref, c_ref, got_ref, three_ref, four_ref):
    by2 = pooling_matrix(256, 2)
    a, b, c = a_ref[...], b_ref[...], c_ref[...]
    got_ref[pl.ds(0, 128), :] = a
    got_ref[pl.ds(128, 64), :] = b
    got_ref[pl.ds(192, 64), :] = c
    rows = jnp.concatenate([own_ref[...], pool(a, 2, by2[:64, :128]), b, c], axis=0)
    three = pool(rows, 2, by2)
    three_ref[...] = three
    four_ref[...] = pool(three, 2, by2[:64, :128])


def pair_kernel(four_ref, three_ref, fours_ref, fives_ref):
    by2 = pooling_matrix(128, 2)
    fours = jnp.concatenate([four_ref[...], pool(three_ref[...], 2, by2)], axis=0)
    fours_ref[...] = fours
    fives_ref[...] = pool(fours, 2, by2)


def times(a, b, dims):
    return lax.dot_general(a, b, (dims, ((), ())), preferred_element_type=jnp.float32)


def attend_kernel(plan, carried, final, *refs):
    refs = list(refs)
    bias = refs.pop(0)[0]
    q_ref = refs.pop(0)
    arrays = [refs.pop(0) for _ in range(1 + max(max(p[0], p[1]) for p in plan))]
    if carried:
        acc_in, m_in, l_in = refs.pop(0), refs.pop(0), refs.pop(0)

    def one_head(h, _):
        def lanes(first):
            return pl.ds(pl.multiple_of(first + h * HD, HD), HD)

        def put(rows, acc, peak, total):
            if final:
                refs[0][rows, lanes(0)] = (acc * (1.0 / total)).astype(jnp.bfloat16).T
            else:
                refs[0][h, :, rows] = acc
                refs[1][h, :, rows] = peak
                refs[2][h, :, rows] = total

        pieces = []
        for k_at, v_at, first, count, v_lane, masked in plan:
            rows = pl.ds(first, count)
            pieces.append((arrays[k_at][rows, lanes(0)], arrays[v_at][rows, lanes(v_lane)].T, masked))

        query = q_ref[:, lanes(0)]
        acc, total = 0.0, 0.0
        if carried:
            acc, peak, total = acc_in[h], m_in[h], l_in[h]
            parts = pieces
        else:
            (k, v, masked), *rest = pieces
            parts = [(k[:256], v[:, :256], masked), (k[256:], v[:, 256:], masked), *rest]
            peak = None
        for k, v, masked in parts:
            s = times(k, query, ((1,), (1,)))
            if masked:
                s = s + bias
            if peak is None:
                peak = jnp.max(s, axis=0, keepdims=True)
            p = jnp.exp2((s - peak) * SCALE_LOG2)
            total = total + jnp.sum(p, axis=0, keepdims=True)
            acc = acc + times(v, p.astype(jnp.bfloat16), ((1,), (0,)))
        put(pl.ds(0, TOK), acc, peak, total)

        @pl.when(jnp.logical_not(jnp.max(total) < TOTAL_LIMIT))
        def _():
            def one_tile(tile, _):
                rows = pl.ds(pl.multiple_of(tile * Q_TILE, Q_TILE), Q_TILE)
                query = q_ref[rows, lanes(0)]
                scores = []
                for k, _, masked in pieces:
                    s = times(k, query, ((1,), (1,)))
                    scores.append(s + bias if masked else s)
                peaks = [jnp.max(s, axis=0, keepdims=True) for s in scores]
                acc, total = 0.0, 0.0
                if carried:
                    before = m_in[h, :, rows]
                    peaks.append(before)
                peak = functools.reduce(jnp.maximum, peaks)
                if carried:
                    fade = jnp.exp2((before - peak) * SCALE_LOG2)
                    acc, total = acc_in[h, :, rows] * fade, l_in[h, :, rows] * fade
                for s, (_, v, _) in zip(scores, pieces):
                    p = jnp.exp2((s - peak) * SCALE_LOG2)
                    total = total + jnp.sum(p, axis=0, keepdims=True)
                    acc = acc + times(v, p.astype(jnp.bfloat16), ((1,), (0,)))
                put(rows, acc, peak, total)
                return 0

            lax.fori_loop(0, TOK // Q_TILE, one_tile, 0)

        return 0

    lax.fori_loop(0, HEADS_DEV, one_head, 0)


def attend(bias, queries, arrays, plan, state, final):
    vmem = pl.BlockSpec(memory_space=pltpu.VMEM)
    operands = [bias, queries, *arrays, *state]
    count = sum(piece[3] for piece in plan)
    if final:
        out_specs = vmem
        out_shape = jax.ShapeDtypeStruct((TOK, WIDTH), jnp.bfloat16)
    else:
        out_specs = [vmem] * 3
        out_shape = [
            jax.ShapeDtypeStruct((HEADS_DEV, rows, TOK), jnp.float32) for rows in (HD, 1, 1)
        ]
    return pl.pallas_call(
        functools.partial(attend_kernel, plan, bool(state), final),
        in_specs=[pl.BlockSpec(memory_space=pltpu.SMEM)] + [vmem] * (len(operands) - 1),
        out_specs=out_specs,
        out_shape=out_shape,
        compiler_params=pltpu.CompilerParams(vmem_limit_bytes=VMEM_LIMIT),
        cost_estimate=pl.CostEstimate(
            flops=4 * TOK * count * WIDTH,
            bytes_accessed=2 * TOK * WIDTH + 4 * count * WIDTH + 4 * TOK * WIDTH,
            transcendentals=TOK * count * HEADS_DEV,
        ),
    )(*operands)


def on_device(queries, keys, values):
    position = lax.axis_index("ctx")
    core = (position % 2).astype(jnp.int32).reshape(1)
    outer = (position == 0) | (position == N_CTX - 1)
    bias = jnp.where(outer, jnp.float32(-1e30), jnp.float32(0)).reshape(1)

    near, far, one, two = first_pools(core, keys, values)
    got2 = swap(two, along_y(2))
    got1 = swap(one, along_y(1))
    got3 = swap(two, along_y(3))
    near_got = swap(near, other_core)
    own = (0, 1, 0, TOK, 0, False)
    state = attend(bias, queries, [keys, values], (own,), (), False)

    planes, three, four = small_call(plane_kernel, (256, 128, 64), two, got1, got2, got3)
    three_got = swap(three, along_z(1))
    far_got = swap(far, beside)
    planes_got = swap(planes, other_core)
    plan = ((0, 0, 0, 512, WIDTH, False), (1, 1, 0, 256, WIDTH, False))
    state = attend(bias, queries, [near_got, planes], plan, state, False)

    fours, fives = small_call(pair_kernel, (128, 64), four, three_got)
    fives5 = swap(fives, along_z(5))
    fours2 = swap(fours, along_z(2))
    fives6 = swap(fives, along_z(6))
    plan = ((0, 0, 0, 256, WIDTH, False), (1, 1, 0, 256, WIDTH, True))
    state = attend(bias, queries, [planes_got, far_got], plan, state, False)

    upper = jnp.concatenate([three_got, fives5, fives6, fours2], axis=0)
    upper_got = swap(upper, other_core)
    plan = ((0, 0, 0, 384, WIDTH, False),)
    state = attend(bias, queries, [upper], plan, state, False)
    return attend(bias, queries, [upper_got], plan, state, True)


def solution(mesh):
    return jax.shard_map(
        on_device,
        mesh=mesh,
        in_specs=(P("ctx", "head"), P("ctx", "head"), P("ctx", "head")),
        out_specs=P("ctx", "head"),
        check_vma=False,
    )
```

```python
import functools

import jax
import jax.numpy as jnp
from jax import lax
from jax.experimental import pallas as pl
from jax.experimental.pallas import tpu as pltpu
from jax.sharding import PartitionSpec as P


HD = 128
HEADS_DEV = 4
WIDTH = HEADS_DEV * HD
TOK = 1024
POOL = 256
EDGE = 256
N_CTX = 64
SCALE_LOG2 = (HD**-0.5) * 1.4426950408889634
Q_TILE = 128
BLOCK = 256
TOTAL_LIMIT = 2.0**100
VMEM_LIMIT = 24 * 2**20


def swap(value, partner):
    pairs = []
    for source in range(N_CTX):
        z, y, core = source // 8, (source // 2) % 4, source % 2
        target = partner(z, y, core)
        if target is not None:
            pairs.append((source, target))
    return lax.ppermute(value, "ctx", pairs)


def index_of(z, y, core):
    return (z * 4 + y) * 2 + core


def other_core(z, y, core):
    return index_of(z, y, 1 - core)


def along_y(bits):
    return lambda z, y, core: index_of(z, y ^ bits, core)


def along_z(bits):
    return lambda z, y, core: index_of(z ^ bits, y, core)


def beside(z, y, core):
    here = index_of(z, y, core)
    there = here + 1 if core else here - 1
    return there if 0 <= there < N_CTX else None


def pooling_matrix(rows, group):
    out = lax.broadcasted_iota(jnp.int32, (rows // group, rows), 0)
    src = lax.broadcasted_iota(jnp.int32, (rows // group, rows), 1)
    return (src // group == out).astype(jnp.float32).astype(jnp.bfloat16)


def pool(value, group, matrix):
    total = jnp.dot(matrix, value, preferred_element_type=jnp.float32)
    return (total / jnp.float32(group**0.5)).astype(jnp.bfloat16)


def first_kernel(core_ref, k_hbm, v_hbm, near_ref, far_ref, one_ref, two_ref, buf, sems):
    core = core_ref[0]
    by4 = pooling_matrix(BLOCK, 4)
    by2 = pooling_matrix(BLOCK // 4, 2)
    copies = []
    for part in range(TOK // BLOCK):
        rows = pl.ds(part * BLOCK, BLOCK)
        for side, ref in enumerate((k_hbm, v_hbm)):
            there = buf.at[rows, pl.ds(side * WIDTH, WIDTH)]
            copies.append(pltpu.make_async_copy(ref.at[rows, :], there, sems.at[2 * part + side]))
    for copy in copies:
        copy.start()
    for part in range(TOK // BLOCK):
        for side in range(2):
            copies[2 * part + side].wait()
            cols = pl.ds(side * WIDTH, WIDTH)
            zero = pool(buf[pl.ds(part * BLOCK, BLOCK), cols], 4, by4)
            one = pool(zero, 2, by2)
            near_ref[pl.ds(part * (BLOCK // 4), BLOCK // 4), cols] = zero
            one_ref[pl.ds(part * (BLOCK // 8), BLOCK // 8), cols] = one
            two = pool(one, 2, by2[: BLOCK // 16, : BLOCK // 8])
            two_ref[pl.ds(part * (BLOCK // 16), BLOCK // 16), cols] = two
    last = pl.multiple_of((1 - core) * (TOK - EDGE), EDGE)
    near_ref[pl.ds(POOL, EDGE), :] = buf[pl.ds(last, EDGE), :]
    first = pl.multiple_of(core * (TOK - EDGE), EDGE)
    far_ref[...] = buf[pl.ds(first, EDGE), :]


def first_pools(core, keys, values):
    counts = (POOL + EDGE, EDGE, POOL // 2, POOL // 4)
    hbm = pl.BlockSpec(memory_space=pltpu.HBM)
    return pl.pallas_call(
        first_kernel,
        in_specs=[pl.BlockSpec(memory_space=pltpu.SMEM), hbm, hbm],
        out_specs=[pl.BlockSpec(memory_space=pltpu.VMEM)] * 4,
        out_shape=[jax.ShapeDtypeStruct((r, 2 * WIDTH), jnp.bfloat16) for r in counts],
        scratch_shapes=[
            pltpu.VMEM((TOK, 2 * WIDTH), jnp.bfloat16),
            pltpu.SemaphoreType.DMA((2 * TOK // BLOCK,)),
        ],
        compiler_params=pltpu.CompilerParams(vmem_limit_bytes=VMEM_LIMIT),
        cost_estimate=pl.CostEstimate(flops=10**8, bytes_accessed=4 * 2**20, transcendentals=0),
        name="first_pools",
    )(core, keys, values)


def small_call(kernel, rows, *operands):
    vmem = pl.BlockSpec(memory_space=pltpu.VMEM)
    return pl.pallas_call(
        kernel,
        in_specs=[vmem] * len(operands),
        out_specs=[vmem] * len(rows),
        out_shape=[jax.ShapeDtypeStruct((r, 2 * WIDTH), jnp.bfloat16) for r in rows],
        compiler_params=pltpu.CompilerParams(vmem_limit_bytes=VMEM_LIMIT),
        cost_estimate=pl.CostEstimate(flops=10**8, bytes_accessed=2**20, transcendentals=0),
    )(*operands)


def plane_kernel(own_ref, a_ref, b_ref, c_ref, got_ref, three_ref, four_ref):
    by2 = pooling_matrix(256, 2)
    a, b, c = a_ref[...], b_ref[...], c_ref[...]
    got_ref[pl.ds(0, 128), :] = a
    got_ref[pl.ds(128, 64), :] = b
    got_ref[pl.ds(192, 64), :] = c
    rows = jnp.concatenate([own_ref[...], pool(a, 2, by2[:64, :128]), b, c], axis=0)
    three = pool(rows, 2, by2)
    three_ref[...] = three
    four_ref[...] = pool(three, 2, by2[:64, :128])


def pair_kernel(near_ref, planes_ref, four_ref, three_ref, fours_ref, fives_ref, chip_ref):
    by2 = pooling_matrix(128, 2)
    three = three_ref[...]
    fours = jnp.concatenate([four_ref[...], pool(three, 2, by2)], axis=0)
    fours_ref[...] = fours
    fives_ref[...] = pool(fours, 2, by2)
    chip_ref[pl.ds(0, 512), :] = near_ref[...]
    chip_ref[pl.ds(512, 256), :] = planes_ref[...]
    chip_ref[pl.ds(768, 128), :] = three


def times(a, b, dims):
    return lax.dot_general(a, b, (dims, ((), ())), preferred_element_type=jnp.float32)


def attend_kernel(plan, carried, final, fetched, *refs):
    refs = list(refs)
    bias = refs.pop(0)[0]
    q_ref = refs.pop(0)
    arrays = [refs.pop(0) for _ in range(1 + max(max(p[0], p[1]) for p in plan))]
    if carried:
        acc_in, m_in, l_in = refs.pop(0), refs.pop(0), refs.pop(0)
    if fetched:
        sems = refs.pop()
        held = [refs.pop(-2), refs.pop()]

        def fetch(at, h):
            lanes = pl.ds(pl.multiple_of(h * HD, HD), HD)
            there = held[at].at[:, lanes]
            return pltpu.make_async_copy(arrays[at].at[:, lanes], there, sems.at[at, h])

        for h in range(HEADS_DEV):
            for at in range(2):
                fetch(at, h).start()

    def one_head(h, _):
        def lanes(first):
            return pl.ds(pl.multiple_of(first + h * HD, HD), HD)

        sources = arrays
        if fetched:
            for at in range(2):
                fetch(at, h).wait()
            sources = held

        def put(rows, acc, peak, total):
            if final:
                refs[0][rows, lanes(0)] = (acc * (1.0 / total)).astype(jnp.bfloat16).T
            else:
                refs[0][h, :, rows] = acc
                refs[1][h, :, rows] = peak
                refs[2][h, :, rows] = total

        pieces = []
        for k_at, v_at, first, count, v_lane, masked in plan:
            rows = pl.ds(first, count)
            k, v = sources[k_at][rows, lanes(0)], sources[v_at][rows, lanes(v_lane)]
            pieces.append((k, v.T, masked))

        query = q_ref[:, lanes(0)]
        acc, total = 0.0, 0.0
        if carried:
            acc, peak, total = acc_in[h], m_in[h], l_in[h]
            parts = pieces
        else:
            (k, v, masked), *rest = pieces
            parts = [(k[:256], v[:, :256], masked), (k[256:], v[:, 256:], masked), *rest]
            peak = None
        for k, v, masked in parts:
            s = times(k, query, ((1,), (1,)))
            if masked:
                s = s + bias
            if peak is None:
                peak = jnp.max(s, axis=0, keepdims=True)
            p = jnp.exp2((s - peak) * SCALE_LOG2)
            total = total + jnp.sum(p, axis=0, keepdims=True)
            acc = acc + times(v, p.astype(jnp.bfloat16), ((1,), (0,)))
        put(pl.ds(0, TOK), acc, peak, total)

        @pl.when(jnp.logical_not(jnp.max(total) < TOTAL_LIMIT))
        def _():
            def one_tile(tile, _):
                rows = pl.ds(pl.multiple_of(tile * Q_TILE, Q_TILE), Q_TILE)
                query = q_ref[rows, lanes(0)]
                scores = []
                for k, _, masked in pieces:
                    s = times(k, query, ((1,), (1,)))
                    scores.append(s + bias if masked else s)
                peaks = [jnp.max(s, axis=0, keepdims=True) for s in scores]
                acc, total = 0.0, 0.0
                if carried:
                    before = m_in[h, :, rows]
                    peaks.append(before)
                peak = functools.reduce(jnp.maximum, peaks)
                if carried:
                    fade = jnp.exp2((before - peak) * SCALE_LOG2)
                    acc, total = acc_in[h, :, rows] * fade, l_in[h, :, rows] * fade
                for s, (_, v, _) in zip(scores, pieces):
                    p = jnp.exp2((s - peak) * SCALE_LOG2)
                    total = total + jnp.sum(p, axis=0, keepdims=True)
                    acc = acc + times(v, p.astype(jnp.bfloat16), ((1,), (0,)))
                put(rows, acc, peak, total)
                return 0

            lax.fori_loop(0, TOK // Q_TILE, one_tile, 0)

        return 0

    lax.fori_loop(0, HEADS_DEV, one_head, 0)


def attend(bias, queries, arrays, plan, state, final, fetched=False):
    vmem = pl.BlockSpec(memory_space=pltpu.VMEM)
    operands = [bias, queries, *arrays, *state]
    count = sum(piece[3] for piece in plan)
    around, scratch = [vmem] * len(arrays), []
    if fetched:
        around = [pl.BlockSpec(memory_space=pltpu.HBM)] * len(arrays)
        scratch = [pltpu.VMEM(array.shape, array.dtype) for array in arrays]
        scratch.append(pltpu.SemaphoreType.DMA((len(arrays), HEADS_DEV)))
    if final:
        out_specs = vmem
        out_shape = jax.ShapeDtypeStruct((TOK, WIDTH), jnp.bfloat16)
    else:
        out_specs = [vmem] * 3
        out_shape = [
            jax.ShapeDtypeStruct((HEADS_DEV, rows, TOK), jnp.float32) for rows in (HD, 1, 1)
        ]
    return pl.pallas_call(
        functools.partial(attend_kernel, plan, bool(state), final, fetched),
        in_specs=[pl.BlockSpec(memory_space=pltpu.SMEM), vmem, *around, *[vmem] * len(state)],
        scratch_shapes=scratch,
        out_specs=out_specs,
        out_shape=out_shape,
        compiler_params=pltpu.CompilerParams(vmem_limit_bytes=VMEM_LIMIT),
        cost_estimate=pl.CostEstimate(
            flops=4 * TOK * count * WIDTH,
            bytes_accessed=2 * TOK * WIDTH + 4 * count * WIDTH + 4 * TOK * WIDTH,
            transcendentals=TOK * count * HEADS_DEV,
        ),
    )(*operands)


def on_device(queries, keys, values):
    position = lax.axis_index("ctx")
    core = (position % 2).astype(jnp.int32).reshape(1)
    outer = (position == 0) | (position == N_CTX - 1)
    bias = jnp.where(outer, jnp.float32(-1e30), jnp.float32(0)).reshape(1)

    keys = pltpu.with_memory_space_constraint(keys, pltpu.HBM)
    values = pltpu.with_memory_space_constraint(values, pltpu.HBM)
    near, far, one, two = first_pools(core, keys, values)
    got1 = swap(one, along_y(1))
    got2 = swap(two, along_y(2))
    got3 = swap(two, along_y(3))
    plan = ((0, 1, 0, TOK, 0, False),)
    state = attend(bias, queries, [keys, values], plan, (), False, fetched=True)

    planes, three, four = small_call(plane_kernel, (256, 128, 64), two, got1, got2, got3)
    three_got = swap(three, along_z(1))
    far_got = swap(far, beside)
    plan = ((0, 0, 0, 256, WIDTH, False),)
    state = attend(bias, queries, [planes], plan, state, False)

    fours, fives, chip = small_call(pair_kernel, (128, 64, 896), near, planes, four, three_got)
    fours2 = swap(fours, along_z(2))
    fives5 = swap(fives, along_z(5))
    fives6 = swap(fives, along_z(6))
    chip_got = swap(chip, other_core)
    plan = ((0, 0, 0, 896, WIDTH, False),)
    plan += ((1, 1, 0, 128, WIDTH, False), (2, 2, 0, 256, WIDTH, True))
    state = attend(bias, queries, [chip_got, three_got, far_got], plan, state, False)

    upper = jnp.concatenate([fours2, fives5, fives6], axis=0)
    upper_got = swap(upper, other_core)
    plan = ((0, 0, 0, 256, WIDTH, False),)
    state = attend(bias, queries, [upper], plan, state, False)
    return attend(bias, queries, [upper_got], plan, state, True)


def solution(mesh):
    return jax.shard_map(
        on_device,
        mesh=mesh,
        in_specs=(P("ctx", "head"), P("ctx", "head"), P("ctx", "head")),
        out_specs=P("ctx", "head"),
        check_vma=False,
    )
```

```python
import functools

import jax
import jax.numpy as jnp
from jax import lax
from jax.experimental import pallas as pl
from jax.experimental.pallas import tpu as pltpu
from jax.sharding import PartitionSpec as P


HD = 128
HEADS_DEV = 4
WIDTH = HEADS_DEV * HD
TOK = 1024
POOL = 256
EDGE = 256
N_CTX = 64
SCALE_LOG2 = (HD**-0.5) * 1.4426950408889634
Q_TILE = 128
BLOCK = 256
TOTAL_LIMIT = 2.0**100
VMEM_LIMIT = 24 * 2**20


def swap(value, partner):
    pairs = []
    for source in range(N_CTX):
        z, y, core = source // 8, (source // 2) % 4, source % 2
        target = partner(z, y, core)
        if target is not None:
            pairs.append((source, target))
    return lax.ppermute(value, "ctx", pairs)


def index_of(z, y, core):
    return (z * 4 + y) * 2 + core


def other_core(z, y, core):
    return index_of(z, y, 1 - core)


def along_y(bits):
    return lambda z, y, core: index_of(z, y ^ bits, core)


def along_z(first, second):
    return lambda z, y, core: index_of(z ^ (second if core else first), y, core)


def beside(z, y, core):
    here = index_of(z, y, core)
    there = here + 1 if core else here - 1
    return there if 0 <= there < N_CTX else None


def pooling_matrix(rows, group):
    out = lax.broadcasted_iota(jnp.int32, (rows // group, rows), 0)
    src = lax.broadcasted_iota(jnp.int32, (rows // group, rows), 1)
    return (src // group == out).astype(jnp.float32).astype(jnp.bfloat16)


def pool(value, group, matrix):
    total = jnp.dot(matrix, value, preferred_element_type=jnp.float32)
    return (total / jnp.float32(group**0.5)).astype(jnp.bfloat16)


def first_kernel(core_ref, k_hbm, v_hbm, near_ref, far_ref, one_ref, two_ref, buf, sems):
    core = core_ref[0]
    by4 = pooling_matrix(BLOCK, 4)
    by2 = pooling_matrix(POOL, 2)
    copies = []
    for part in range(TOK // BLOCK):
        rows = pl.ds(part * BLOCK, BLOCK)
        for side, ref in enumerate((k_hbm, v_hbm)):
            there = buf.at[rows, pl.ds(side * WIDTH, WIDTH)]
            copies.append(pltpu.make_async_copy(ref.at[rows, :], there, sems.at[2 * part + side]))
    for copy in copies:
        copy.start()
    for part in range(TOK // BLOCK):
        for side in range(2):
            copies[2 * part + side].wait()
            cols = pl.ds(side * WIDTH, WIDTH)
            zero = pool(buf[pl.ds(part * BLOCK, BLOCK), cols], 4, by4)
            near_ref[pl.ds(part * (BLOCK // 4), BLOCK // 4), cols] = zero
    one = pool(near_ref[pl.ds(0, POOL), :], 2, by2)
    one_ref[...] = one
    two_ref[...] = pool(one, 2, by2[: POOL // 4, : POOL // 2])
    last = pl.multiple_of((1 - core) * (TOK - EDGE), EDGE)
    near_ref[pl.ds(POOL, EDGE), :] = buf[pl.ds(last, EDGE), :]
    first = pl.multiple_of(core * (TOK - EDGE), EDGE)
    far_ref[...] = buf[pl.ds(first, EDGE), :]


def first_pools(core, keys, values):
    counts = (POOL + EDGE, EDGE, POOL // 2, POOL // 4)
    hbm = pl.BlockSpec(memory_space=pltpu.HBM)
    return pl.pallas_call(
        first_kernel,
        in_specs=[pl.BlockSpec(memory_space=pltpu.SMEM), hbm, hbm],
        out_specs=[pl.BlockSpec(memory_space=pltpu.VMEM)] * 4,
        out_shape=[jax.ShapeDtypeStruct((r, 2 * WIDTH), jnp.bfloat16) for r in counts],
        scratch_shapes=[
            pltpu.VMEM((TOK, 2 * WIDTH), jnp.bfloat16),
            pltpu.SemaphoreType.DMA((2 * TOK // BLOCK,)),
        ],
        compiler_params=pltpu.CompilerParams(vmem_limit_bytes=VMEM_LIMIT),
        cost_estimate=pl.CostEstimate(flops=10**8, bytes_accessed=4 * 2**20, transcendentals=0),
        name="first_pools",
    )(core, keys, values)


def small_call(kernel, rows, *operands):
    vmem = pl.BlockSpec(memory_space=pltpu.VMEM)
    return pl.pallas_call(
        kernel,
        in_specs=[vmem] * len(operands),
        out_specs=[vmem] * len(rows),
        out_shape=[jax.ShapeDtypeStruct((r, 2 * WIDTH), jnp.bfloat16) for r in rows],
        compiler_params=pltpu.CompilerParams(vmem_limit_bytes=VMEM_LIMIT),
        cost_estimate=pl.CostEstimate(flops=10**8, bytes_accessed=2**20, transcendentals=0),
    )(*operands)


def plane_kernel(own_ref, a_ref, b_ref, c_ref, got_ref, three_ref):
    by2 = pooling_matrix(256, 2)
    a, b, c = a_ref[...], b_ref[...], c_ref[...]
    own = own_ref[...]
    got_ref[pl.ds(0, 128), :] = a
    got_ref[pl.ds(128, 64), :] = b
    got_ref[pl.ds(192, 64), :] = c
    got_ref[pl.ds(256, 64), :] = own
    rows = jnp.concatenate([pool(a, 2, by2[:64, :128]), b, c, own], axis=0)
    three_ref[...] = pool(rows, 2, by2)


def wide_kernel(three_ref, got_ref, fours_ref, fives_ref):
    by2 = pooling_matrix(256, 2)
    rows = jnp.concatenate(
        [pool(got_ref[pl.ds(0, 128), :], 2, by2[:64, :128]), got_ref[pl.ds(128, 192), :]], axis=0
    )
    threes = jnp.concatenate([three_ref[...], pool(rows, 2, by2)], axis=0)
    fours = pool(threes, 2, by2)
    fours_ref[...] = fours
    fives_ref[...] = pool(fours, 2, by2[:64, :128])


def times(a, b, dims):
    return lax.dot_general(a, b, (dims, ((), ())), preferred_element_type=jnp.float32)


def attend_kernel(plan, carried, final, fetched, *refs):
    refs = list(refs)
    bias = refs.pop(0)[0]
    q_ref = refs.pop(0)
    arrays = [refs.pop(0) for _ in range(1 + max(max(p[0], p[1]) for p in plan))]
    if carried:
        acc_in, m_in, l_in = refs.pop(0), refs.pop(0), refs.pop(0)
    if fetched:
        sems = refs.pop()
        held = [refs.pop(-2), refs.pop()]

        def fetch(at, h):
            lanes = pl.ds(pl.multiple_of(h * HD, HD), HD)
            there = held[at].at[:, lanes]
            return pltpu.make_async_copy(arrays[at].at[:, lanes], there, sems.at[at, h])

        for h in range(HEADS_DEV):
            for at in range(2):
                fetch(at, h).start()

    def one_head(h, _):
        def lanes(first):
            return pl.ds(pl.multiple_of(first + h * HD, HD), HD)

        sources = arrays
        if fetched:
            for at in range(2):
                fetch(at, h).wait()
            sources = held

        def put(rows, acc, peak, total):
            if final:
                refs[0][rows, lanes(0)] = (acc * (1.0 / total)).astype(jnp.bfloat16).T
            else:
                refs[0][h, :, rows] = acc
                refs[1][h, :, rows] = peak
                refs[2][h, :, rows] = total

        pieces = []
        for k_at, v_at, first, count, v_lane, masked in plan:
            rows = pl.ds(first, count)
            k, v = sources[k_at][rows, lanes(0)], sources[v_at][rows, lanes(v_lane)]
            pieces.append((k, v.T, masked))

        query = q_ref[:, lanes(0)]
        acc, total = 0.0, 0.0
        if carried:
            acc, peak, total = acc_in[h], m_in[h], l_in[h]
            parts = pieces
        else:
            (k, v, masked), *rest = pieces
            parts = [(k[:256], v[:, :256], masked), (k[256:], v[:, 256:], masked), *rest]
            peak = None
        for k, v, masked in parts:
            s = times(k, query, ((1,), (1,)))
            if masked:
                s = s + bias
            if peak is None:
                peak = jnp.max(s, axis=0, keepdims=True)
            p = jnp.exp2((s - peak) * SCALE_LOG2)
            total = total + jnp.sum(p, axis=0, keepdims=True)
            acc = acc + times(v, p.astype(jnp.bfloat16), ((1,), (0,)))
        put(pl.ds(0, TOK), acc, peak, total)

        @pl.when(jnp.logical_not(jnp.max(total) < TOTAL_LIMIT))
        def _():
            def one_tile(tile, _):
                rows = pl.ds(pl.multiple_of(tile * Q_TILE, Q_TILE), Q_TILE)
                query = q_ref[rows, lanes(0)]
                scores = []
                for k, _, masked in pieces:
                    s = times(k, query, ((1,), (1,)))
                    scores.append(s + bias if masked else s)
                peaks = [jnp.max(s, axis=0, keepdims=True) for s in scores]
                acc, total = 0.0, 0.0
                if carried:
                    before = m_in[h, :, rows]
                    peaks.append(before)
                peak = functools.reduce(jnp.maximum, peaks)
                if carried:
                    fade = jnp.exp2((before - peak) * SCALE_LOG2)
                    acc, total = acc_in[h, :, rows] * fade, l_in[h, :, rows] * fade
                for s, (_, v, _) in zip(scores, pieces):
                    p = jnp.exp2((s - peak) * SCALE_LOG2)
                    total = total + jnp.sum(p, axis=0, keepdims=True)
                    acc = acc + times(v, p.astype(jnp.bfloat16), ((1,), (0,)))
                put(rows, acc, peak, total)
                return 0

            lax.fori_loop(0, TOK // Q_TILE, one_tile, 0)

        return 0

    lax.fori_loop(0, HEADS_DEV, one_head, 0)


def attend(bias, queries, arrays, plan, state, final, fetched=False):
    vmem = pl.BlockSpec(memory_space=pltpu.VMEM)
    operands = [bias, queries, *arrays, *state]
    count = sum(piece[3] for piece in plan)
    around, scratch = [vmem] * len(arrays), []
    if fetched:
        around = [pl.BlockSpec(memory_space=pltpu.HBM)] * len(arrays)
        scratch = [pltpu.VMEM(array.shape, array.dtype) for array in arrays]
        scratch.append(pltpu.SemaphoreType.DMA((len(arrays), HEADS_DEV)))
    if final:
        out_specs = vmem
        out_shape = jax.ShapeDtypeStruct((TOK, WIDTH), jnp.bfloat16)
    else:
        out_specs = [vmem] * 3
        out_shape = [
            jax.ShapeDtypeStruct((HEADS_DEV, rows, TOK), jnp.float32) for rows in (HD, 1, 1)
        ]
    return pl.pallas_call(
        functools.partial(attend_kernel, plan, bool(state), final, fetched),
        in_specs=[pl.BlockSpec(memory_space=pltpu.SMEM), vmem, *around, *[vmem] * len(state)],
        scratch_shapes=scratch,
        out_specs=out_specs,
        out_shape=out_shape,
        compiler_params=pltpu.CompilerParams(vmem_limit_bytes=VMEM_LIMIT),
        cost_estimate=pl.CostEstimate(
            flops=4 * TOK * count * WIDTH,
            bytes_accessed=2 * TOK * WIDTH + 4 * count * WIDTH + 4 * TOK * WIDTH,
            transcendentals=TOK * count * HEADS_DEV,
        ),
    )(*operands)


def on_device(queries, keys, values):
    position = lax.axis_index("ctx")
    core = (position % 2).astype(jnp.int32).reshape(1)
    outer = (position == 0) | (position == N_CTX - 1)
    bias = jnp.where(outer, jnp.float32(-1e30), jnp.float32(0)).reshape(1)

    keys = pltpu.with_memory_space_constraint(keys, pltpu.HBM)
    values = pltpu.with_memory_space_constraint(values, pltpu.HBM)
    near, far, one, two = first_pools(core, keys, values)
    got1 = swap(one, along_y(1))
    got2 = swap(two, along_y(2))
    got3 = swap(two, along_y(3))
    near_got = swap(near, other_core)
    plan = ((0, 1, 0, TOK, 0, False),)
    state = attend(bias, queries, [keys, values], plan, (), False, fetched=True)

    planes, three = small_call(plane_kernel, (320, 128), two, got1, got2, got3)
    planes_got = swap(planes, other_core)
    three_got = swap(three, along_z(1, 1))
    fours, fives = small_call(wide_kernel, (128, 64), three, planes_got)
    fours_got = swap(fours, along_z(2, 3))
    far_got = swap(far, beside)
    fives_c = swap(fives, along_z(5, 4))
    fives_d = swap(fives, along_z(6, 7))
    plan = ((0, 0, 0, 512, WIDTH, False), (1, 1, 0, 256, WIDTH, False))
    plan += ((2, 2, 0, 256, WIDTH, False),)
    state = attend(bias, queries, [near_got, planes, planes_got], plan, state, False)

    upper = jnp.concatenate([three_got, fours_got, fives_c, fives_d], axis=0)
    upper_got = swap(upper, other_core)
    plan = ((0, 0, 0, 384, WIDTH, False), (1, 1, 0, 256, WIDTH, True))
    state = attend(bias, queries, [upper, far_got], plan, state, False)
    plan = ((0, 0, 0, 384, WIDTH, False),)
    return attend(bias, queries, [upper_got], plan, state, True)


def solution(mesh):
    return jax.shard_map(
        on_device,
        mesh=mesh,
        in_specs=(P("ctx", "head"), P("ctx", "head"), P("ctx", "head")),
        out_specs=P("ctx", "head"),
        check_vma=False,
    )
```

```python
import functools

import jax
import jax.numpy as jnp
from jax import lax
from jax.experimental import pallas as pl
from jax.experimental.pallas import tpu as pltpu
from jax.sharding import PartitionSpec as P


HD = 128
HEADS_DEV = 4
WIDTH = HEADS_DEV * HD
TOK = 1024
POOL = 256
EDGE = 256
N_CTX = 64
SCALE_LOG2 = (HD**-0.5) * 1.4426950408889634
Q_TILE = 128
STRIP = 1024
BLOCK = 256
TOTAL_LIMIT = 2.0**100
VMEM_LIMIT = 24 * 2**20


def swap(value, partner):
    pairs = []
    for source in range(N_CTX):
        z, y, core = source // 8, (source // 2) % 4, source % 2
        target = partner(z, y, core)
        if target is not None:
            pairs.append((source, target))
    return lax.ppermute(value, "ctx", pairs)


def index_of(z, y, core):
    return (z * 4 + y) * 2 + core


def other_core(z, y, core):
    return index_of(z, y, 1 - core)


def along_y(first, second):
    return lambda z, y, core: index_of(z, y ^ (second if core else first), core)


def along_z(first, second):
    return lambda z, y, core: index_of(z ^ (second if core else first), y, core)


def beside(z, y, core):
    here = index_of(z, y, core)
    there = here + 1 if core else here - 1
    return there if 0 <= there < N_CTX else None


def pooling_matrix(rows, group):
    out = lax.broadcasted_iota(jnp.int32, (rows // group, rows), 0)
    src = lax.broadcasted_iota(jnp.int32, (rows // group, rows), 1)
    return (src // group == out).astype(jnp.float32).astype(jnp.bfloat16)


def pool(value, group, matrix):
    total = jnp.dot(matrix, value, preferred_element_type=jnp.float32)
    return (total / jnp.float32(group**0.5)).astype(jnp.bfloat16)


def first_kernel(core_ref, k_hbm, v_hbm, near_ref, far_hbm, one_ref, two_ref, buf, sems, far_sem):
    core = core_ref[0]
    by4 = pooling_matrix(BLOCK, 4)
    by2 = pooling_matrix(POOL, 2)
    copies = []
    for part in range(TOK // BLOCK):
        rows = pl.ds(part * BLOCK, BLOCK)
        for side, ref in enumerate((k_hbm, v_hbm)):
            there = buf.at[rows, pl.ds(side * WIDTH, WIDTH)]
            copies.append(pltpu.make_async_copy(ref.at[rows, :], there, sems.at[2 * part + side]))
    for copy in copies:
        copy.start()
    for part in range(TOK // BLOCK):
        for side in range(2):
            copies[2 * part + side].wait()
            cols = pl.ds(side * WIDTH, WIDTH)
            zero = pool(buf[pl.ds(part * BLOCK, BLOCK), cols], 4, by4)
            near_ref[pl.ds(part * (BLOCK // 4), BLOCK // 4), cols] = zero
    first = pl.multiple_of(core * (TOK - EDGE), EDGE)
    far = pltpu.make_async_copy(buf.at[pl.ds(first, EDGE), :], far_hbm, far_sem)
    far.start()
    one = pool(near_ref[pl.ds(0, POOL), :], 2, by2)
    one_ref[...] = one
    two = pool(one, 2, by2[: POOL // 4, : POOL // 2])
    two_ref[...] = two
    near_ref[pl.ds(POOL + EDGE, POOL // 4), :] = two
    last = pl.multiple_of((1 - core) * (TOK - EDGE), EDGE)
    near_ref[pl.ds(POOL, EDGE), :] = buf[pl.ds(last, EDGE), :]
    far.wait()


def first_pools(core, keys, values):
    counts = (POOL + EDGE + POOL // 4, EDGE, POOL // 2, POOL // 4)
    hbm, vmem = (pl.BlockSpec(memory_space=m) for m in (pltpu.HBM, pltpu.VMEM))
    return pl.pallas_call(
        first_kernel,
        in_specs=[pl.BlockSpec(memory_space=pltpu.SMEM), hbm, hbm],
        out_specs=[vmem, hbm, vmem, vmem],
        out_shape=[
            (pltpu.HBM if r == EDGE else jax.ShapeDtypeStruct)((r, 2 * WIDTH), jnp.bfloat16)
            for r in counts
        ],
        scratch_shapes=[
            pltpu.VMEM((TOK, 2 * WIDTH), jnp.bfloat16),
            pltpu.SemaphoreType.DMA((2 * TOK // BLOCK,)),
            pltpu.SemaphoreType.DMA,
        ],
        compiler_params=pltpu.CompilerParams(vmem_limit_bytes=VMEM_LIMIT),
        cost_estimate=pl.CostEstimate(flops=10**8, bytes_accessed=4 * 2**20, transcendentals=0),
        name="first_pools",
    )(core, keys, values)


def small_call(kernel, rows, *operands):
    vmem = pl.BlockSpec(memory_space=pltpu.VMEM)
    return pl.pallas_call(
        kernel,
        in_specs=[vmem] * len(operands),
        out_specs=[vmem] * len(rows),
        out_shape=[jax.ShapeDtypeStruct((r, 2 * WIDTH), jnp.bfloat16) for r in rows],
        compiler_params=pltpu.CompilerParams(vmem_limit_bytes=VMEM_LIMIT),
        cost_estimate=pl.CostEstimate(flops=10**8, bytes_accessed=2**20, transcendentals=0),
    )(*operands)


def both_kernel(two_ref, near_ref, both_ref):
    both_ref[pl.ds(0, 64), :] = two_ref[...]
    both_ref[pl.ds(64, 64), :] = near_ref[pl.ds(512, 64), :]


def threes(two, one_got, twos_got, by2):
    rows = jnp.concatenate([pool(one_got, 2, by2[:64, :128]), twos_got, two], axis=0)
    return pool(rows, 2, by2)


def plane_kernel(two_ref, one_ref, twos_ref, got_ref, three_ref):
    one, twos = one_ref[...], twos_ref[...]
    got_ref[pl.ds(0, 128), :] = one
    got_ref[pl.ds(128, 128), :] = twos
    three_ref[...] = threes(two_ref[...], one, twos, pooling_matrix(256, 2))


def wide_kernel(three_ref, got_ref, near_ref, fours_ref, fives_ref):
    by2 = pooling_matrix(256, 2)
    got = got_ref[pl.ds(0, 128), :], got_ref[pl.ds(128, 128), :]
    other = threes(near_ref[pl.ds(512, 64), :], *got, by2)
    fours = pool(jnp.concatenate([three_ref[...], other], axis=0), 2, by2)
    fours_ref[...] = fours
    fives_ref[...] = pool(fours, 2, by2[:64, :128])


def times(a, b, dims):
    return lax.dot_general(a, b, (dims, ((), ())), preferred_element_type=jnp.float32)


def attend_kernel(plan, carried, final, fetched, *refs):
    refs = list(refs)
    bias = refs.pop(0)[0]
    q_ref = refs.pop(0)
    arrays = [refs.pop(0) for _ in range(1 + max(max(p[0], p[1]) for p in plan))]
    if carried:
        acc_in, m_in, l_in = refs.pop(0), refs.pop(0), refs.pop(0)
    if fetched:
        sems = refs.pop()
        held = [refs.pop(-2), refs.pop()]

        def fetch(at, h):
            lanes = pl.ds(pl.multiple_of(h * HD, HD), HD)
            there = held[at].at[:, lanes]
            return pltpu.make_async_copy(arrays[at].at[:, lanes], there, sems.at[at, h])

        for h in range(HEADS_DEV):
            for at in range(2):
                fetch(at, h).start()

    sources = held if fetched else arrays

    def lanes(first, h):
        if isinstance(h, int):
            return pl.ds(first + h * HD, HD)
        return pl.ds(pl.multiple_of(first + h * HD, HD), HD)

    def pieces_of(h):
        pieces = []
        for k_at, v_at, first, count, v_lane, masked in plan:
            rows = pl.ds(first, count)
            k, v = sources[k_at][rows, lanes(0, h)], sources[v_at][rows, lanes(v_lane, h)]
            pieces.append((k, v.T, masked))
        return pieces

    def put(h, rows, acc, peak, total):
        if final:
            refs[0][rows, lanes(0, h)] = (acc * (1.0 / total)).astype(jnp.bfloat16).T
        else:
            refs[0][h, :, rows] = acc
            refs[1][h, :, rows] = peak
            refs[2][h, :, rows] = total

    def add(v, s, peak, total, acc):
        p = jnp.exp2((s - peak) * SCALE_LOG2)
        total = total + jnp.sum(p, axis=0, keepdims=True)
        return total, acc + times(v, p.astype(jnp.bfloat16), ((1,), (0,)))

    largest = []
    for h in range(HEADS_DEV):
        if fetched:
            for at in range(2):
                fetch(at, h).wait()
        pieces = pieces_of(h)
        for first in range(0, TOK, STRIP):
            rows = pl.ds(first, STRIP)
            query = q_ref[rows, lanes(0, h)]
            acc, total = 0.0, 0.0
            if carried:
                acc, peak, total = acc_in[h, :, rows], m_in[h, :, rows], l_in[h, :, rows]
                parts = pieces
            else:
                (k, v, masked), *rest = pieces
                parts = [(k[:256], v[:, :256], masked), (k[256:], v[:, 256:], masked), *rest]
                peak = None
            for k, v, masked in parts:
                s = times(k, query, ((1,), (1,)))
                if masked:
                    s = s + bias
                if peak is None:
                    peak = jnp.max(s, axis=0, keepdims=True)
                total, acc = add(v, s, peak, total, acc)
            put(h, rows, acc, peak, total)
            largest.append(jnp.max(total, axis=1, keepdims=True))

    @pl.when(jnp.logical_not(jnp.max(functools.reduce(jnp.maximum, largest)) < TOTAL_LIMIT))
    def _():
        def one_tile(index, _):
            h = index // (TOK // Q_TILE)
            rows = pl.ds(pl.multiple_of(index % (TOK // Q_TILE) * Q_TILE, Q_TILE), Q_TILE)
            query = q_ref[rows, lanes(0, h)]
            pieces = pieces_of(h)
            scores = []
            for k, _, masked in pieces:
                s = times(k, query, ((1,), (1,)))
                scores.append(s + bias if masked else s)
            peaks = [jnp.max(s, axis=0, keepdims=True) for s in scores]
            acc, total = 0.0, 0.0
            if carried:
                before = m_in[h, :, rows]
                peaks.append(before)
            peak = functools.reduce(jnp.maximum, peaks)
            if carried:
                fade = jnp.exp2((before - peak) * SCALE_LOG2)
                acc, total = acc_in[h, :, rows] * fade, l_in[h, :, rows] * fade
            for s, (k, v, _) in zip(scores, pieces):
                total, acc = add(v, s, peak, total, acc)
            put(h, rows, acc, peak, total)
            return 0

        lax.fori_loop(0, HEADS_DEV * (TOK // Q_TILE), one_tile, 0)


def attend(bias, queries, arrays, plan, state, final, fetched=False):
    vmem = pl.BlockSpec(memory_space=pltpu.VMEM)
    operands = [bias, queries, *arrays, *state]
    count = sum(piece[3] for piece in plan)
    around, scratch = [vmem] * len(arrays), []
    if fetched:
        around = [pl.BlockSpec(memory_space=pltpu.HBM)] * len(arrays)
        scratch = [pltpu.VMEM(array.shape, array.dtype) for array in arrays]
        scratch.append(pltpu.SemaphoreType.DMA((len(arrays), HEADS_DEV)))
    if final:
        out_specs = vmem
        out_shape = jax.ShapeDtypeStruct((TOK, WIDTH), jnp.bfloat16)
    else:
        out_specs = [vmem] * 3
        out_shape = [
            jax.ShapeDtypeStruct((HEADS_DEV, rows, TOK), jnp.float32) for rows in (HD, 1, 1)
        ]
    return pl.pallas_call(
        functools.partial(attend_kernel, plan, bool(state), final, fetched),
        in_specs=[pl.BlockSpec(memory_space=pltpu.SMEM), vmem, *around, *[vmem] * len(state)],
        scratch_shapes=scratch,
        out_specs=out_specs,
        out_shape=out_shape,
        compiler_params=pltpu.CompilerParams(vmem_limit_bytes=VMEM_LIMIT),
        cost_estimate=pl.CostEstimate(
            flops=4 * TOK * count * WIDTH,
            bytes_accessed=2 * TOK * WIDTH + 4 * count * WIDTH + 4 * TOK * WIDTH,
            transcendentals=TOK * count * HEADS_DEV,
        ),
    )(*operands)


def on_device(queries, keys, values):
    position = lax.axis_index("ctx")
    core = (position % 2).astype(jnp.int32).reshape(1)
    outer = (position == 0) | (position == N_CTX - 1)
    bias = jnp.where(outer, jnp.float32(-1e30), jnp.float32(0)).reshape(1)

    keys = pltpu.with_memory_space_constraint(keys, pltpu.HBM)
    values = pltpu.with_memory_space_constraint(values, pltpu.HBM)
    near, far, one, two = first_pools(core, keys, values)
    near_got = swap(near, other_core)
    one_got = swap(one, along_y(1, 1))
    (both,) = small_call(both_kernel, (128,), two, near_got)
    twos_got = swap(both, along_y(2, 3))
    plan = ((0, 1, 0, TOK, 0, False),)
    state = attend(bias, queries, [keys, values], plan, (), False, fetched=True)

    planes, three = small_call(plane_kernel, (256, 128), two, one_got, twos_got)
    planes_got = swap(planes, other_core)
    three_got = swap(three, along_z(1, 1))
    fours, fives = small_call(wide_kernel, (128, 64), three, planes_got, near_got)
    fours_got = swap(fours, along_z(2, 3))
    far_got = swap(far, beside)
    fives_c = swap(fives, along_z(5, 4))
    fives_d = swap(fives, along_z(6, 7))
    plan = ((0, 0, 0, 512, WIDTH, False), (1, 1, 0, 256, WIDTH, False))
    plan += ((2, 2, 0, 256, WIDTH, False),)
    state = attend(bias, queries, [near_got, planes, planes_got], plan, state, False)

    upper = jnp.concatenate([three_got, fours_got, fives_c, fives_d], axis=0)
    upper_got = swap(upper, other_core)
    plan = ((0, 0, 0, 384, WIDTH, False), (1, 1, 0, 256, WIDTH, True))
    state = attend(bias, queries, [upper, far_got], plan, state, False)
    plan = ((0, 0, 0, 384, WIDTH, False),)
    return attend(bias, queries, [upper_got], plan, state, True)


def solution(mesh):
    return jax.shard_map(
        on_device,
        mesh=mesh,
        in_specs=(P("ctx", "head"), P("ctx", "head"), P("ctx", "head")),
        out_specs=P("ctx", "head"),
        check_vma=False,
    )
```

```python
import functools

import jax
import jax.numpy as jnp
from jax import lax
from jax.experimental import pallas as pl
from jax.experimental.pallas import tpu as pltpu
from jax.sharding import PartitionSpec as P


HD = 128
HEADS_DEV = 4
WIDTH = HEADS_DEV * HD
TOK = 1024
POOL = 256
EDGE = 256
N_CTX = 64
SCALE_LOG2 = (HD**-0.5) * 1.4426950408889634
Q_TILE = 128
STRIP = 1024
BLOCK = 256
TOTAL_LIMIT = 2.0**100
VMEM_LIMIT = 24 * 2**20


def swap(value, partner):
    pairs = []
    for source in range(N_CTX):
        z, y, core = source // 8, (source // 2) % 4, source % 2
        target = partner(z, y, core)
        if target is not None:
            pairs.append((source, target))
    return lax.ppermute(value, "ctx", pairs)


def index_of(z, y, core):
    return (z * 4 + y) * 2 + core


def other_core(z, y, core):
    return index_of(z, y, 1 - core)


def along_y(first, second):
    return lambda z, y, core: index_of(z, y ^ (second if core else first), core)


def along_z(first, second):
    return lambda z, y, core: index_of(z ^ (second if core else first), y, core)


def beside(z, y, core):
    here = index_of(z, y, core)
    there = here + 1 if core else here - 1
    return there if 0 <= there < N_CTX else None


def pooling_matrix(rows, group):
    out = lax.broadcasted_iota(jnp.int32, (rows // group, rows), 0)
    src = lax.broadcasted_iota(jnp.int32, (rows // group, rows), 1)
    return (src // group == out).astype(jnp.float32).astype(jnp.bfloat16)


def pool(value, group, matrix):
    total = jnp.dot(matrix, value, preferred_element_type=jnp.float32)
    return (total / jnp.float32(group**0.5)).astype(jnp.bfloat16)


def first_kernel(core_ref, k_hbm, v_hbm, near_ref, far_hbm, one_ref, two_ref, buf, sems, far_sem):
    core = core_ref[0]
    by4 = pooling_matrix(BLOCK, 4)
    by2 = pooling_matrix(POOL, 2)
    copies = []
    for part in range(TOK // BLOCK):
        rows = pl.ds(part * BLOCK, BLOCK)
        for side, ref in enumerate((k_hbm, v_hbm)):
            there = buf.at[rows, pl.ds(side * WIDTH, WIDTH)]
            copies.append(pltpu.make_async_copy(ref.at[rows, :], there, sems.at[2 * part + side]))
    for copy in copies:
        copy.start()
    for part in range(TOK // BLOCK):
        for side in range(2):
            copies[2 * part + side].wait()
            cols = pl.ds(side * WIDTH, WIDTH)
            zero = pool(buf[pl.ds(part * BLOCK, BLOCK), cols], 4, by4)
            near_ref[pl.ds(part * (BLOCK // 4), BLOCK // 4), cols] = zero
    first = pl.multiple_of(core * (TOK - EDGE), EDGE)
    far = pltpu.make_async_copy(buf.at[pl.ds(first, EDGE), :], far_hbm, far_sem)
    far.start()
    one = pool(near_ref[pl.ds(0, POOL), :], 2, by2)
    one_ref[...] = one
    two = pool(one, 2, by2[: POOL // 4, : POOL // 2])
    two_ref[...] = two
    near_ref[pl.ds(POOL + EDGE, POOL // 4), :] = two
    last = pl.multiple_of((1 - core) * (TOK - EDGE), EDGE)
    near_ref[pl.ds(POOL, EDGE), :] = buf[pl.ds(last, EDGE), :]
    far.wait()


def first_pools(core, keys, values):
    counts = (POOL + EDGE + POOL // 4, EDGE, POOL // 2, POOL // 4)
    hbm, vmem = (pl.BlockSpec(memory_space=m) for m in (pltpu.HBM, pltpu.VMEM))
    return pl.pallas_call(
        first_kernel,
        in_specs=[pl.BlockSpec(memory_space=pltpu.SMEM), hbm, hbm],
        out_specs=[vmem, hbm, vmem, vmem],
        out_shape=[
            (pltpu.HBM if r == EDGE else jax.ShapeDtypeStruct)((r, 2 * WIDTH), jnp.bfloat16)
            for r in counts
        ],
        scratch_shapes=[
            pltpu.VMEM((TOK, 2 * WIDTH), jnp.bfloat16),
            pltpu.SemaphoreType.DMA((2 * TOK // BLOCK,)),
            pltpu.SemaphoreType.DMA,
        ],
        compiler_params=pltpu.CompilerParams(vmem_limit_bytes=VMEM_LIMIT),
        cost_estimate=pl.CostEstimate(flops=10**8, bytes_accessed=4 * 2**20, transcendentals=0),
        name="first_pools",
    )(core, keys, values)


def small_call(kernel, rows, *operands):
    vmem = pl.BlockSpec(memory_space=pltpu.VMEM)
    return pl.pallas_call(
        kernel,
        in_specs=[vmem] * len(operands),
        out_specs=[vmem] * len(rows),
        out_shape=[jax.ShapeDtypeStruct((r, 2 * WIDTH), jnp.bfloat16) for r in rows],
        compiler_params=pltpu.CompilerParams(vmem_limit_bytes=VMEM_LIMIT),
        cost_estimate=pl.CostEstimate(flops=10**8, bytes_accessed=2**20, transcendentals=0),
    )(*operands)


def both_kernel(two_ref, near_ref, both_ref):
    both_ref[pl.ds(0, 64), :] = two_ref[...]
    both_ref[pl.ds(64, 64), :] = near_ref[pl.ds(512, 64), :]


def threes(two, one_got, twos_got, by2):
    rows = jnp.concatenate([pool(one_got, 2, by2[:64, :128]), twos_got, two], axis=0)
    return pool(rows, 2, by2)


def plane_kernel(two_ref, one_ref, twos_ref, got_ref, three_ref):
    one, twos = one_ref[...], twos_ref[...]
    got_ref[pl.ds(0, 128), :] = one
    got_ref[pl.ds(128, 128), :] = twos
    three_ref[...] = threes(two_ref[...], one, twos, pooling_matrix(256, 2))


def wide_kernel(three_ref, got_ref, near_ref, fours_ref, fives_ref):
    by2 = pooling_matrix(256, 2)
    got = got_ref[pl.ds(0, 128), :], got_ref[pl.ds(128, 128), :]
    other = threes(near_ref[pl.ds(512, 64), :], *got, by2)
    fours = pool(jnp.concatenate([three_ref[...], other], axis=0), 2, by2)
    fours_ref[...] = fours
    fives_ref[...] = pool(fours, 2, by2[:64, :128])


def times(a, b, dims):
    return lax.dot_general(a, b, (dims, ((), ())), preferred_element_type=jnp.float32)


def attend_kernel(plan, carried, final, fetched, *refs):
    refs = list(refs)
    bias = refs.pop(0)[0]
    q_ref = refs.pop(0)
    arrays = [refs.pop(0) for _ in range(1 + max(max(p[0], p[1]) for p in plan))]
    if carried:
        acc_in, m_in, l_in = refs.pop(0), refs.pop(0), refs.pop(0)
    if fetched:
        sems = refs.pop()
        held = [refs.pop(-2), refs.pop()]

        def fetch(at, h):
            lanes = pl.ds(pl.multiple_of(h * HD, HD), HD)
            there = held[at].at[:, lanes]
            return pltpu.make_async_copy(arrays[at].at[:, lanes], there, sems.at[at, h])

        for h in range(HEADS_DEV):
            for at in range(2):
                fetch(at, h).start()

    sources = held if fetched else arrays

    def lanes(first, h):
        if isinstance(h, int):
            return pl.ds(first + h * HD, HD)
        return pl.ds(pl.multiple_of(first + h * HD, HD), HD)

    def pieces_of(h):
        pieces = []
        for k_at, v_at, first, count, v_lane, masked in plan:
            rows = pl.ds(first, count)
            k, v = sources[k_at][rows, lanes(0, h)], sources[v_at][rows, lanes(v_lane, h)]
            pieces.append((k, v.T, masked))
        return pieces

    def put(h, rows, acc, peak, total):
        if final:
            refs[0][rows, lanes(0, h)] = (acc * (1.0 / total)).astype(jnp.bfloat16).T
        else:
            refs[0][h, :, rows] = acc
            refs[1][h, :, rows] = peak
            refs[2][h, :, rows] = total

    def add(v, s, peak, total, acc):
        p = jnp.exp2((s - peak) * SCALE_LOG2)
        total = total + jnp.sum(p, axis=0, keepdims=True)
        return total, acc + times(v, p.astype(jnp.bfloat16), ((1,), (0,)))

    largest = []
    for h in range(HEADS_DEV):
        if fetched:
            for at in range(2):
                fetch(at, h).wait()
        pieces = pieces_of(h)
        for first in range(0, TOK, STRIP):
            rows = pl.ds(first, STRIP)
            query = q_ref[rows, lanes(0, h)]
            acc, total = 0.0, 0.0
            if carried:
                acc, peak, total = acc_in[h, :, rows], m_in[h, :, rows], l_in[h, :, rows]
                parts = pieces
            else:
                (k, v, masked), *rest = pieces
                parts = [(k[:256], v[:, :256], masked), (k[256:], v[:, 256:], masked), *rest]
                peak = None
            for k, v, masked in parts:
                s = times(k, query, ((1,), (1,)))
                if masked:
                    s = s + bias
                if peak is None:
                    peak = jnp.max(s, axis=0, keepdims=True)
                total, acc = add(v, s, peak, total, acc)
            put(h, rows, acc, peak, total)
            largest.append(jnp.max(total, axis=1, keepdims=True))

    @pl.when(jnp.logical_not(jnp.max(functools.reduce(jnp.maximum, largest)) < TOTAL_LIMIT))
    def _():
        def one_tile(index, _):
            h = index // (TOK // Q_TILE)
            rows = pl.ds(pl.multiple_of(index % (TOK // Q_TILE) * Q_TILE, Q_TILE), Q_TILE)
            query = q_ref[rows, lanes(0, h)]
            pieces = pieces_of(h)
            scores = []
            for k, _, masked in pieces:
                s = times(k, query, ((1,), (1,)))
                scores.append(s + bias if masked else s)
            peaks = [jnp.max(s, axis=0, keepdims=True) for s in scores]
            acc, total = 0.0, 0.0
            if carried:
                before = m_in[h, :, rows]
                peaks.append(before)
            peak = functools.reduce(jnp.maximum, peaks)
            if carried:
                fade = jnp.exp2((before - peak) * SCALE_LOG2)
                acc, total = acc_in[h, :, rows] * fade, l_in[h, :, rows] * fade
            for s, (k, v, _) in zip(scores, pieces):
                total, acc = add(v, s, peak, total, acc)
            put(h, rows, acc, peak, total)
            return 0

        lax.fori_loop(0, HEADS_DEV * (TOK // Q_TILE), one_tile, 0)


def attend(bias, queries, arrays, plan, state, final, fetched=False):
    vmem = pl.BlockSpec(memory_space=pltpu.VMEM)
    operands = [bias, queries, *arrays, *state]
    count = sum(piece[3] for piece in plan)
    around, scratch = [vmem] * len(arrays), []
    if fetched:
        around = [pl.BlockSpec(memory_space=pltpu.HBM)] * len(arrays)
        scratch = [pltpu.VMEM(array.shape, array.dtype) for array in arrays]
        scratch.append(pltpu.SemaphoreType.DMA((len(arrays), HEADS_DEV)))
    if final:
        out_specs = vmem
        out_shape = jax.ShapeDtypeStruct((TOK, WIDTH), jnp.bfloat16)
    else:
        out_specs = [vmem] * 3
        out_shape = [
            jax.ShapeDtypeStruct((HEADS_DEV, rows, TOK), jnp.float32) for rows in (HD, 1, 1)
        ]
    return pl.pallas_call(
        functools.partial(attend_kernel, plan, bool(state), final, fetched),
        in_specs=[pl.BlockSpec(memory_space=pltpu.SMEM), vmem, *around, *[vmem] * len(state)],
        scratch_shapes=scratch,
        out_specs=out_specs,
        out_shape=out_shape,
        compiler_params=pltpu.CompilerParams(vmem_limit_bytes=VMEM_LIMIT),
        cost_estimate=pl.CostEstimate(
            flops=4 * TOK * count * WIDTH,
            bytes_accessed=2 * TOK * WIDTH + 4 * count * WIDTH + 4 * TOK * WIDTH,
            transcendentals=TOK * count * HEADS_DEV,
        ),
    )(*operands)


def on_device(queries, keys, values):
    position = lax.axis_index("ctx")
    core = (position % 2).astype(jnp.int32).reshape(1)
    outer = (position == 0) | (position == N_CTX - 1)
    bias = jnp.where(outer, jnp.float32(-1e30), jnp.float32(0)).reshape(1)

    keys = pltpu.with_memory_space_constraint(keys, pltpu.HBM)
    values = pltpu.with_memory_space_constraint(values, pltpu.HBM)
    near, far, one, two = first_pools(core, keys, values)
    one_got = swap(one, along_y(1, 1))
    near_got = swap(near, other_core)
    (both,) = small_call(both_kernel, (128,), two, near_got)
    twos_got = swap(both, along_y(2, 3))
    plan = ((0, 1, 0, TOK, 0, False),)
    state = attend(bias, queries, [keys, values], plan, (), False, fetched=True)
    plan = ((0, 0, 0, 512, WIDTH, False),)
    state = attend(bias, queries, [near_got], plan, state, False)

    planes, three = small_call(plane_kernel, (256, 128), two, one_got, twos_got)
    planes_got = swap(planes, other_core)
    three_got = swap(three, along_z(1, 1))
    fours, fives = small_call(wide_kernel, (128, 64), three, planes_got, near_got)
    fours_got = swap(fours, along_z(2, 3))
    fives_c = swap(fives, along_z(5, 4))
    fives_d = swap(fives, along_z(6, 7))
    far_got = swap(far, beside)
    plan = ((0, 0, 0, 256, WIDTH, False), (1, 1, 0, 256, WIDTH, False))
    state = attend(bias, queries, [planes, planes_got], plan, state, False)

    upper = jnp.concatenate([three_got, fours_got, fives_c, fives_d], axis=0)
    upper_got = swap(upper, other_core)
    plan = ((0, 0, 0, 384, WIDTH, False),)
    state = attend(bias, queries, [upper], plan, state, False)
    plan += ((1, 1, 0, 256, WIDTH, True),)
    return attend(bias, queries, [upper_got, far_got], plan, state, True)


def solution(mesh):
    return jax.shard_map(
        on_device,
        mesh=mesh,
        in_specs=(P("ctx", "head"), P("ctx", "head"), P("ctx", "head")),
        out_specs=P("ctx", "head"),
        check_vma=False,
    )
```

```python
import functools

import jax
import jax.numpy as jnp
from jax import lax
from jax.experimental import pallas as pl
from jax.experimental.pallas import tpu as pltpu
from jax.sharding import PartitionSpec as P


HD = 128
HEADS_DEV = 4
WIDTH = HEADS_DEV * HD
TOK = 1024
POOL = 256
EDGE = 256
N_CTX = 64
SCALE_LOG2 = (HD**-0.5) * 1.4426950408889634
Q_TILE = 128
STRIP = 1024
BLOCK = 256
TOTAL_LIMIT = 2.0**100
VMEM_LIMIT = 24 * 2**20


def swap(value, partner):
    pairs = []
    for source in range(N_CTX):
        z, y, core = source // 8, (source // 2) % 4, source % 2
        target = partner(z, y, core)
        if target is not None:
            pairs.append((source, target))
    return lax.ppermute(value, "ctx", pairs)


def index_of(z, y, core):
    return (z * 4 + y) * 2 + core


def other_core(z, y, core):
    return index_of(z, y, 1 - core)


def along_y(first, second):
    return lambda z, y, core: index_of(z, y ^ (second if core else first), core)


def along_z(first, second):
    return lambda z, y, core: index_of(z ^ (second if core else first), y, core)


def beside(z, y, core):
    here = index_of(z, y, core)
    there = here + 1 if core else here - 1
    return there if 0 <= there < N_CTX else None


def pooling_matrix(rows, group):
    out = lax.broadcasted_iota(jnp.int32, (rows // group, rows), 0)
    src = lax.broadcasted_iota(jnp.int32, (rows // group, rows), 1)
    return (src // group == out).astype(jnp.float32).astype(jnp.bfloat16)


def pool(value, group, matrix):
    total = jnp.dot(matrix, value, preferred_element_type=jnp.float32)
    return (total / jnp.float32(group**0.5)).astype(jnp.bfloat16)


def first_kernel(core_ref, k_hbm, v_hbm, near_ref, far_hbm, one_ref, two_ref, buf, sems, far_sem):
    core = core_ref[0]
    by4 = pooling_matrix(BLOCK, 4)
    by2 = pooling_matrix(POOL, 2)
    copies = []
    for part in range(TOK // BLOCK):
        rows = pl.ds(part * BLOCK, BLOCK)
        for side, ref in enumerate((k_hbm, v_hbm)):
            there = buf.at[rows, pl.ds(side * WIDTH, WIDTH)]
            copies.append(pltpu.make_async_copy(ref.at[rows, :], there, sems.at[2 * part + side]))
    for copy in copies:
        copy.start()
    for part in range(TOK // BLOCK):
        for side in range(2):
            copies[2 * part + side].wait()
            cols = pl.ds(side * WIDTH, WIDTH)
            zero = pool(buf[pl.ds(part * BLOCK, BLOCK), cols], 4, by4)
            near_ref[pl.ds(part * (BLOCK // 4), BLOCK // 4), cols] = zero
    first = pl.multiple_of(core * (TOK - EDGE), EDGE)
    far = pltpu.make_async_copy(buf.at[pl.ds(first, EDGE), :], far_hbm, far_sem)
    far.start()
    one = pool(near_ref[pl.ds(0, POOL), :], 2, by2)
    one_ref[...] = one
    two = pool(one, 2, by2[: POOL // 4, : POOL // 2])
    two_ref[...] = two
    near_ref[pl.ds(POOL + EDGE, POOL // 4), :] = two
    last = pl.multiple_of((1 - core) * (TOK - EDGE), EDGE)
    near_ref[pl.ds(POOL, EDGE), :] = buf[pl.ds(last, EDGE), :]
    far.wait()


def first_pools(core, keys, values):
    counts = (POOL + EDGE + POOL // 4, EDGE, POOL // 2, POOL // 4)
    hbm, vmem = (pl.BlockSpec(memory_space=m) for m in (pltpu.HBM, pltpu.VMEM))
    return pl.pallas_call(
        first_kernel,
        in_specs=[pl.BlockSpec(memory_space=pltpu.SMEM), hbm, hbm],
        out_specs=[vmem, hbm, vmem, vmem],
        out_shape=[
            (pltpu.HBM if r == EDGE else pltpu.VMEM)((r, 2 * WIDTH), jnp.bfloat16) for r in counts
        ],
        scratch_shapes=[
            pltpu.VMEM((TOK, 2 * WIDTH), jnp.bfloat16),
            pltpu.SemaphoreType.DMA((2 * TOK // BLOCK,)),
            pltpu.SemaphoreType.DMA,
        ],
        compiler_params=pltpu.CompilerParams(vmem_limit_bytes=VMEM_LIMIT),
        cost_estimate=pl.CostEstimate(flops=10**8, bytes_accessed=4 * 2**20, transcendentals=0),
        name="first_pools",
    )(core, keys, values)


def small_call(kernel, rows, *operands):
    vmem = pl.BlockSpec(memory_space=pltpu.VMEM)
    return pl.pallas_call(
        kernel,
        in_specs=[vmem] * len(operands),
        out_specs=[vmem] * len(rows),
        out_shape=[jax.ShapeDtypeStruct((r, 2 * WIDTH), jnp.bfloat16) for r in rows],
        compiler_params=pltpu.CompilerParams(vmem_limit_bytes=VMEM_LIMIT),
        cost_estimate=pl.CostEstimate(flops=10**8, bytes_accessed=2**20, transcendentals=0),
    )(*operands)


def both_kernel(two_ref, near_ref, both_ref):
    both_ref[pl.ds(0, 64), :] = two_ref[...]
    both_ref[pl.ds(64, 64), :] = near_ref[pl.ds(512, 64), :]


def threes(two, one_got, twos_got, by2):
    rows = jnp.concatenate([pool(one_got, 2, by2[:64, :128]), twos_got, two], axis=0)
    return pool(rows, 2, by2)


def plane_kernel(two_ref, one_ref, twos_ref, got_ref, three_ref):
    one, twos = one_ref[...], twos_ref[...]
    got_ref[pl.ds(0, 128), :] = one
    got_ref[pl.ds(128, 128), :] = twos
    three_ref[...] = threes(two_ref[...], one, twos, pooling_matrix(256, 2))


def wide_kernel(three_ref, got_ref, both_ref, fours_ref, fives_ref):
    by2 = pooling_matrix(256, 2)
    got = got_ref[pl.ds(0, 128), :], got_ref[pl.ds(128, 128), :]
    other = threes(both_ref[pl.ds(64, 64), :], *got, by2)
    fours = pool(jnp.concatenate([three_ref[...], other], axis=0), 2, by2)
    fours_ref[...] = fours
    fives_ref[...] = pool(fours, 2, by2[:64, :128])


def times(a, b, dims):
    return lax.dot_general(a, b, (dims, ((), ())), preferred_element_type=jnp.float32)


def attend_kernel(plan, carried, final, fetched, *refs):
    refs = list(refs)
    bias = refs.pop(0)[0]
    q_ref = refs.pop(0)
    arrays = [refs.pop(0) for _ in range(1 + max(max(p[0], p[1]) for p in plan))]
    if carried:
        acc_in, m_in, l_in = refs.pop(0), refs.pop(0), refs.pop(0)
    if fetched:
        sems = refs.pop()
        held = [refs.pop(-2), refs.pop()]

        def fetch(at, h):
            lanes = pl.ds(pl.multiple_of(h * HD, HD), HD)
            there = held[at].at[:, lanes]
            return pltpu.make_async_copy(arrays[at].at[:, lanes], there, sems.at[at, h])

        for h in range(HEADS_DEV):
            for at in range(2):
                fetch(at, h).start()

    sources = held if fetched else arrays

    def lanes(first, h):
        if isinstance(h, int):
            return pl.ds(first + h * HD, HD)
        return pl.ds(pl.multiple_of(first + h * HD, HD), HD)

    def pieces_of(h):
        pieces = []
        for k_at, v_at, first, count, v_lane, masked in plan:
            rows = pl.ds(first, count)
            k, v = sources[k_at][rows, lanes(0, h)], sources[v_at][rows, lanes(v_lane, h)]
            pieces.append((k, v.T, masked))
        return pieces

    def put(h, rows, acc, peak, total):
        if final:
            refs[0][rows, lanes(0, h)] = (acc * (1.0 / total)).astype(jnp.bfloat16).T
        else:
            refs[0][h, :, rows] = acc
            refs[1][h, :, rows] = peak
            refs[2][h, :, rows] = total

    def add(v, s, peak, total, acc):
        p = jnp.exp2((s - peak) * SCALE_LOG2)
        total = total + jnp.sum(p, axis=0, keepdims=True)
        return total, acc + times(v, p.astype(jnp.bfloat16), ((1,), (0,)))

    largest = []
    for h in range(HEADS_DEV):
        if fetched:
            for at in range(2):
                fetch(at, h).wait()
        pieces = pieces_of(h)
        for first in range(0, TOK, STRIP):
            rows = pl.ds(first, STRIP)
            query = q_ref[rows, lanes(0, h)]
            acc, total = 0.0, 0.0
            if carried:
                acc, peak, total = acc_in[h, :, rows], m_in[h, :, rows], l_in[h, :, rows]
                parts = pieces
            else:
                (k, v, masked), *rest = pieces
                parts = [(k[:256], v[:, :256], masked), (k[256:], v[:, 256:], masked), *rest]
                peak = None
            for k, v, masked in parts:
                s = times(k, query, ((1,), (1,)))
                if masked:
                    s = s + bias
                if peak is None:
                    peak = jnp.max(s, axis=0, keepdims=True)
                total, acc = add(v, s, peak, total, acc)
            put(h, rows, acc, peak, total)
            largest.append(jnp.max(total, axis=1, keepdims=True))

    @pl.when(jnp.logical_not(jnp.max(functools.reduce(jnp.maximum, largest)) < TOTAL_LIMIT))
    def _():
        def one_tile(index, _):
            h = index // (TOK // Q_TILE)
            rows = pl.ds(pl.multiple_of(index % (TOK // Q_TILE) * Q_TILE, Q_TILE), Q_TILE)
            query = q_ref[rows, lanes(0, h)]
            pieces = pieces_of(h)
            scores = []
            for k, _, masked in pieces:
                s = times(k, query, ((1,), (1,)))
                scores.append(s + bias if masked else s)
            peaks = [jnp.max(s, axis=0, keepdims=True) for s in scores]
            acc, total = 0.0, 0.0
            if carried:
                before = m_in[h, :, rows]
                peaks.append(before)
            peak = functools.reduce(jnp.maximum, peaks)
            if carried:
                fade = jnp.exp2((before - peak) * SCALE_LOG2)
                acc, total = acc_in[h, :, rows] * fade, l_in[h, :, rows] * fade
            for s, (k, v, _) in zip(scores, pieces):
                total, acc = add(v, s, peak, total, acc)
            put(h, rows, acc, peak, total)
            return 0

        lax.fori_loop(0, HEADS_DEV * (TOK // Q_TILE), one_tile, 0)


def attend(bias, queries, arrays, plan, state, final, fetched=False):
    vmem = pl.BlockSpec(memory_space=pltpu.VMEM)
    operands = [bias, queries, *arrays, *state]
    count = sum(piece[3] for piece in plan)
    around, scratch = [vmem] * len(arrays), []
    if fetched:
        around = [pl.BlockSpec(memory_space=pltpu.HBM)] * len(arrays)
        scratch = [pltpu.VMEM(array.shape, array.dtype) for array in arrays]
        scratch.append(pltpu.SemaphoreType.DMA((len(arrays), HEADS_DEV)))
    if final:
        out_specs = vmem
        out_shape = jax.ShapeDtypeStruct((TOK, WIDTH), jnp.bfloat16)
    else:
        out_specs = [vmem] * 3
        out_shape = [
            jax.ShapeDtypeStruct((HEADS_DEV, rows, TOK), jnp.float32) for rows in (HD, 1, 1)
        ]
    return pl.pallas_call(
        functools.partial(attend_kernel, plan, bool(state), final, fetched),
        in_specs=[pl.BlockSpec(memory_space=pltpu.SMEM), vmem, *around, *[vmem] * len(state)],
        scratch_shapes=scratch,
        out_specs=out_specs,
        out_shape=out_shape,
        compiler_params=pltpu.CompilerParams(vmem_limit_bytes=VMEM_LIMIT),
        cost_estimate=pl.CostEstimate(
            flops=4 * TOK * count * WIDTH,
            bytes_accessed=2 * TOK * WIDTH + 4 * count * WIDTH + 4 * TOK * WIDTH,
            transcendentals=TOK * count * HEADS_DEV,
        ),
    )(*operands)


def on_device(queries, keys, values):
    position = lax.axis_index("ctx")
    core = (position % 2).astype(jnp.int32).reshape(1)
    outer = (position == 0) | (position == N_CTX - 1)
    bias = jnp.where(outer, jnp.float32(-1e30), jnp.float32(0)).reshape(1)

    keys = pltpu.with_memory_space_constraint(keys, pltpu.HBM)
    values = pltpu.with_memory_space_constraint(values, pltpu.HBM)
    near, far, one, two = first_pools(core, keys, values)
    near_got = swap(near, other_core)
    one_got = swap(one, along_y(1, 1))
    (both,) = small_call(both_kernel, (128,), two, near_got)
    twos_got = swap(both, along_y(2, 3))
    plan = ((0, 1, 0, TOK, 0, False),)
    state = attend(bias, queries, [keys, values], plan, (), False, fetched=True)
    plan = ((0, 0, 0, 512, WIDTH, False),)
    state = attend(bias, queries, [near_got], plan, state, False)
    far_got = swap(far, beside)

    planes, three = small_call(plane_kernel, (256, 128), two, one_got, twos_got)
    planes_got = swap(planes, other_core)
    three_got = swap(three, along_z(1, 1))
    fours, fives = small_call(wide_kernel, (128, 64), three, planes_got, both)
    fours_got = swap(fours, along_z(2, 3))
    fives_c = swap(fives, along_z(5, 4))
    fives_d = swap(fives, along_z(6, 7))
    plan = ((0, 0, 0, 256, WIDTH, False), (1, 1, 0, 256, WIDTH, False))
    plan += ((2, 2, 0, 256, WIDTH, True),)
    state = attend(bias, queries, [planes, planes_got, far_got], plan, state, False)

    upper = jnp.concatenate([three_got, fours_got, fives_c, fives_d], axis=0)
    upper_got = swap(upper, other_core)
    plan = ((0, 0, 0, 384, WIDTH, False),)
    state = attend(bias, queries, [upper], plan, state, False)
    return attend(bias, queries, [upper_got], plan, state, True)


def solution(mesh):
    return jax.shard_map(
        on_device,
        mesh=mesh,
        in_specs=(P("ctx", "head"), P("ctx", "head"), P("ctx", "head")),
        out_specs=P("ctx", "head"),
        check_vma=False,
    )
```

```python
import functools

import jax
import jax.numpy as jnp
from jax import lax
from jax.experimental import pallas as pl
from jax.experimental.pallas import tpu as pltpu
from jax.sharding import PartitionSpec as P


HD = 128
HEADS_DEV = 4
WIDTH = HEADS_DEV * HD
TOK = 1024
POOL = 256
EDGE = 256
N_CTX = 64
SCALE_LOG2 = (HD**-0.5) * 1.4426950408889634
Q_TILE = 128
STRIP = 1024
BLOCK = 256
TOTAL_LIMIT = 2.0**100
VMEM_LIMIT = 24 * 2**20


def swap(value, partner):
    pairs = []
    for source in range(N_CTX):
        z, y, core = source // 8, (source // 2) % 4, source % 2
        target = partner(z, y, core)
        if target is not None:
            pairs.append((source, target))
    return lax.ppermute(value, "ctx", pairs)


def index_of(z, y, core):
    return (z * 4 + y) * 2 + core


def other_core(z, y, core):
    return index_of(z, y, 1 - core)


def along_y(first, second):
    return lambda z, y, core: index_of(z, y ^ (second if core else first), core)


def along_z(first, second):
    return lambda z, y, core: index_of(z ^ (second if core else first), y, core)


def beside(z, y, core):
    here = index_of(z, y, core)
    there = here + 1 if core else here - 1
    return there if 0 <= there < N_CTX else None


def pooling_matrix(rows, group):
    out = lax.broadcasted_iota(jnp.int32, (rows // group, rows), 0)
    src = lax.broadcasted_iota(jnp.int32, (rows // group, rows), 1)
    return (src // group == out).astype(jnp.float32).astype(jnp.bfloat16)


def pool(value, group, matrix):
    total = jnp.dot(matrix, value, preferred_element_type=jnp.float32)
    return (total / jnp.float32(group**0.5)).astype(jnp.bfloat16)


def first_kernel(core_ref, k_hbm, v_hbm, near_ref, far_hbm, one_ref, two_ref, buf, sems, far_sem):
    core = core_ref[0]
    by4 = pooling_matrix(BLOCK, 4)
    by2 = pooling_matrix(POOL, 2)
    copies = []
    for part in range(TOK // BLOCK):
        rows = pl.ds(part * BLOCK, BLOCK)
        for side, ref in enumerate((k_hbm, v_hbm)):
            there = buf.at[rows, pl.ds(side * WIDTH, WIDTH)]
            copies.append(pltpu.make_async_copy(ref.at[rows, :], there, sems.at[2 * part + side]))
    for copy in copies:
        copy.start()
    for part in range(TOK // BLOCK):
        for side in range(2):
            copies[2 * part + side].wait()
            cols = pl.ds(side * WIDTH, WIDTH)
            zero = pool(buf[pl.ds(part * BLOCK, BLOCK), cols], 4, by4)
            near_ref[pl.ds(part * (BLOCK // 4), BLOCK // 4), cols] = zero
    first = pl.multiple_of(core * (TOK - EDGE), EDGE)
    far = pltpu.make_async_copy(buf.at[pl.ds(first, EDGE), :], far_hbm, far_sem)
    far.start()
    one = pool(near_ref[pl.ds(0, POOL), :], 2, by2)
    one_ref[...] = one
    two_ref[...] = pool(one, 2, by2[: POOL // 4, : POOL // 2])
    last = pl.multiple_of((1 - core) * (TOK - EDGE), EDGE)
    near_ref[pl.ds(POOL, EDGE), :] = buf[pl.ds(last, EDGE), :]
    far.wait()


def first_pools(core, keys, values):
    counts = (POOL + EDGE, EDGE, POOL // 2, POOL // 4)
    hbm, vmem = (pl.BlockSpec(memory_space=m) for m in (pltpu.HBM, pltpu.VMEM))
    return pl.pallas_call(
        first_kernel,
        in_specs=[pl.BlockSpec(memory_space=pltpu.SMEM), hbm, hbm],
        out_specs=[vmem, hbm, vmem, vmem],
        out_shape=[
            (pltpu.HBM if r == EDGE else pltpu.VMEM)((r, 2 * WIDTH), jnp.bfloat16) for r in counts
        ],
        scratch_shapes=[
            pltpu.VMEM((TOK, 2 * WIDTH), jnp.bfloat16),
            pltpu.SemaphoreType.DMA((2 * TOK // BLOCK,)),
            pltpu.SemaphoreType.DMA,
        ],
        compiler_params=pltpu.CompilerParams(vmem_limit_bytes=VMEM_LIMIT),
        cost_estimate=pl.CostEstimate(flops=10**8, bytes_accessed=4 * 2**20, transcendentals=0),
        name="first_pools",
    )(core, keys, values)


def small_call(kernel, rows, *operands):
    vmem = pl.BlockSpec(memory_space=pltpu.VMEM)
    return pl.pallas_call(
        kernel,
        in_specs=[vmem] * len(operands),
        out_specs=[vmem] * len(rows),
        out_shape=[jax.ShapeDtypeStruct((r, 2 * WIDTH), jnp.bfloat16) for r in rows],
        compiler_params=pltpu.CompilerParams(vmem_limit_bytes=VMEM_LIMIT),
        cost_estimate=pl.CostEstimate(flops=10**8, bytes_accessed=2**20, transcendentals=0),
    )(*operands)


def both_kernel(two_ref, near_ref, both_ref):
    both_ref[pl.ds(0, 64), :] = two_ref[...]
    by2 = pooling_matrix(POOL, 2)
    one = pool(near_ref[pl.ds(0, POOL), :], 2, by2)
    both_ref[pl.ds(64, 64), :] = pool(one, 2, by2[:64, :128])


def threes(two, one_got, twos_got, by2):
    rows = jnp.concatenate([pool(one_got, 2, by2[:64, :128]), twos_got, two], axis=0)
    return pool(rows, 2, by2)


def plane_kernel(two_ref, one_ref, twos_ref, got_ref, three_ref):
    one, twos = one_ref[...], twos_ref[...]
    got_ref[pl.ds(0, 128), :] = one
    got_ref[pl.ds(128, 128), :] = twos
    three_ref[...] = threes(two_ref[...], one, twos, pooling_matrix(256, 2))


def wide_kernel(three_ref, got_ref, both_ref, fours_ref, fives_ref):
    by2 = pooling_matrix(256, 2)
    got = got_ref[pl.ds(0, 128), :], got_ref[pl.ds(128, 128), :]
    other = threes(both_ref[pl.ds(64, 64), :], *got, by2)
    fours = pool(jnp.concatenate([three_ref[...], other], axis=0), 2, by2)
    fours_ref[...] = fours
    fives_ref[...] = pool(fours, 2, by2[:64, :128])


def times(a, b, dims):
    return lax.dot_general(a, b, (dims, ((), ())), preferred_element_type=jnp.float32)


def attend_kernel(plan, carried, final, fetched, *refs):
    refs = list(refs)
    bias = refs.pop(0)[0]
    q_ref = refs.pop(0)
    arrays = [refs.pop(0) for _ in range(1 + max(max(p[0], p[1]) for p in plan))]
    if carried:
        acc_in, m_in, l_in = refs.pop(0), refs.pop(0), refs.pop(0)
    if fetched:
        sems = refs.pop()
        held = [refs.pop(-2), refs.pop()]

        def fetch(at, h):
            lanes = pl.ds(pl.multiple_of(h * HD, HD), HD)
            there = held[at].at[:, lanes]
            return pltpu.make_async_copy(arrays[at].at[:, lanes], there, sems.at[at, h])

        for h in range(HEADS_DEV):
            for at in range(2):
                fetch(at, h).start()

    sources = held if fetched else arrays

    def lanes(first, h):
        if isinstance(h, int):
            return pl.ds(first + h * HD, HD)
        return pl.ds(pl.multiple_of(first + h * HD, HD), HD)

    def pieces_of(h):
        pieces = []
        for k_at, v_at, first, count, v_lane, masked in plan:
            rows = pl.ds(first, count)
            k, v = sources[k_at][rows, lanes(0, h)], sources[v_at][rows, lanes(v_lane, h)]
            pieces.append((k, v.T, masked))
        return pieces

    def put(h, rows, acc, peak, total):
        if final:
            refs[0][rows, lanes(0, h)] = (acc * (1.0 / total)).astype(jnp.bfloat16).T
        else:
            refs[0][h, :, rows] = acc
            refs[1][h, :, rows] = peak
            refs[2][h, :, rows] = total

    def add(v, s, peak, total, acc):
        p = jnp.exp2((s - peak) * SCALE_LOG2)
        total = total + jnp.sum(p, axis=0, keepdims=True)
        return total, acc + times(v, p.astype(jnp.bfloat16), ((1,), (0,)))

    largest = []
    for h in range(HEADS_DEV):
        if fetched:
            for at in range(2):
                fetch(at, h).wait()
        pieces = pieces_of(h)
        for first in range(0, TOK, STRIP):
            rows = pl.ds(first, STRIP)
            query = q_ref[rows, lanes(0, h)]
            acc, total = 0.0, 0.0
            if carried:
                acc, peak, total = acc_in[h, :, rows], m_in[h, :, rows], l_in[h, :, rows]
                parts = pieces
            else:
                (k, v, masked), *rest = pieces
                parts = [(k[:256], v[:, :256], masked), (k[256:], v[:, 256:], masked), *rest]
                peak = None
            for k, v, masked in parts:
                s = times(k, query, ((1,), (1,)))
                if masked:
                    s = s + bias
                if peak is None:
                    peak = jnp.max(s, axis=0, keepdims=True)
                total, acc = add(v, s, peak, total, acc)
            put(h, rows, acc, peak, total)
            largest.append(jnp.max(total, axis=1, keepdims=True))

    @pl.when(jnp.logical_not(jnp.max(functools.reduce(jnp.maximum, largest)) < TOTAL_LIMIT))
    def _():
        def one_tile(index, _):
            h = index // (TOK // Q_TILE)
            rows = pl.ds(pl.multiple_of(index % (TOK // Q_TILE) * Q_TILE, Q_TILE), Q_TILE)
            query = q_ref[rows, lanes(0, h)]
            pieces = pieces_of(h)
            scores = []
            for k, _, masked in pieces:
                s = times(k, query, ((1,), (1,)))
                scores.append(s + bias if masked else s)
            peaks = [jnp.max(s, axis=0, keepdims=True) for s in scores]
            acc, total = 0.0, 0.0
            if carried:
                before = m_in[h, :, rows]
                peaks.append(before)
            peak = functools.reduce(jnp.maximum, peaks)
            if carried:
                fade = jnp.exp2((before - peak) * SCALE_LOG2)
                acc, total = acc_in[h, :, rows] * fade, l_in[h, :, rows] * fade
            for s, (k, v, _) in zip(scores, pieces):
                total, acc = add(v, s, peak, total, acc)
            put(h, rows, acc, peak, total)
            return 0

        lax.fori_loop(0, HEADS_DEV * (TOK // Q_TILE), one_tile, 0)


def attend(bias, queries, arrays, plan, state, final, fetched=False):
    vmem = pl.BlockSpec(memory_space=pltpu.VMEM)
    operands = [bias, queries, *arrays, *state]
    count = sum(piece[3] for piece in plan)
    around, scratch = [vmem] * len(arrays), []
    if fetched:
        around = [pl.BlockSpec(memory_space=pltpu.HBM)] * len(arrays)
        scratch = [pltpu.VMEM(array.shape, array.dtype) for array in arrays]
        scratch.append(pltpu.SemaphoreType.DMA((len(arrays), HEADS_DEV)))
    if final:
        out_specs = vmem
        out_shape = jax.ShapeDtypeStruct((TOK, WIDTH), jnp.bfloat16)
    else:
        out_specs = [vmem] * 3
        out_shape = [
            jax.ShapeDtypeStruct((HEADS_DEV, rows, TOK), jnp.float32) for rows in (HD, 1, 1)
        ]
    return pl.pallas_call(
        functools.partial(attend_kernel, plan, bool(state), final, fetched),
        in_specs=[pl.BlockSpec(memory_space=pltpu.SMEM), vmem, *around, *[vmem] * len(state)],
        scratch_shapes=scratch,
        out_specs=out_specs,
        out_shape=out_shape,
        compiler_params=pltpu.CompilerParams(vmem_limit_bytes=VMEM_LIMIT),
        cost_estimate=pl.CostEstimate(
            flops=4 * TOK * count * WIDTH,
            bytes_accessed=2 * TOK * WIDTH + 4 * count * WIDTH + 4 * TOK * WIDTH,
            transcendentals=TOK * count * HEADS_DEV,
        ),
    )(*operands)


def on_device(queries, keys, values):
    position = lax.axis_index("ctx")
    core = (position % 2).astype(jnp.int32).reshape(1)
    outer = (position == 0) | (position == N_CTX - 1)
    bias = jnp.where(outer, jnp.float32(-1e30), jnp.float32(0)).reshape(1)

    keys = pltpu.with_memory_space_constraint(keys, pltpu.HBM)
    values = pltpu.with_memory_space_constraint(values, pltpu.HBM)
    near, far, one, two = first_pools(core, keys, values)
    near_got = swap(near, other_core)
    one_got = swap(one, along_y(1, 1))
    (both,) = small_call(both_kernel, (128,), two, near_got)
    twos_got = swap(both, along_y(2, 3))
    plan = ((0, 1, 0, TOK, 0, False),)
    state = attend(bias, queries, [keys, values], plan, (), False, fetched=True)
    plan = ((0, 0, 0, 512, WIDTH, False),)
    state = attend(bias, queries, [near_got], plan, state, False)
    far_got = swap(far, beside)

    planes, three = small_call(plane_kernel, (256, 128), two, one_got, twos_got)
    planes_got = swap(planes, other_core)
    three_got = swap(three, along_z(1, 1))
    fours, fives = small_call(wide_kernel, (128, 64), three, planes_got, both)
    fours_got = swap(fours, along_z(2, 3))
    fives_c = swap(fives, along_z(5, 4))
    fives_d = swap(fives, along_z(6, 7))
    plan = ((0, 0, 0, 256, WIDTH, False), (1, 1, 0, 256, WIDTH, False))
    plan += ((2, 2, 0, 256, WIDTH, True),)
    state = attend(bias, queries, [planes, planes_got, far_got], plan, state, False)

    upper = jnp.concatenate([three_got, fours_got, fives_c, fives_d], axis=0)
    upper_got = swap(upper, other_core)
    plan = ((0, 0, 0, 384, WIDTH, False),)
    state = attend(bias, queries, [upper], plan, state, False)
    return attend(bias, queries, [upper_got], plan, state, True)


def solution(mesh):
    return jax.shard_map(
        on_device,
        mesh=mesh,
        in_specs=(P("ctx", "head"), P("ctx", "head"), P("ctx", "head")),
        out_specs=P("ctx", "head"),
        check_vma=False,
    )
```

```python
import functools

import jax
import jax.numpy as jnp
from jax import lax
from jax.experimental import pallas as pl
from jax.experimental.pallas import tpu as pltpu
from jax.sharding import PartitionSpec as P


HD = 128
HEADS_DEV = 4
WIDTH = HEADS_DEV * HD
TOK = 1024
POOL = 256
EDGE = 256
N_CTX = 64
SCALE_LOG2 = (HD**-0.5) * 1.4426950408889634
Q_TILE = 128
STRIP = 1024
BLOCK = 256
TOTAL_LIMIT = 2.0**100
VMEM_LIMIT = 24 * 2**20


def swap(value, partner):
    pairs = []
    for source in range(N_CTX):
        z, y, core = source // 8, (source // 2) % 4, source % 2
        target = partner(z, y, core)
        if target is not None:
            pairs.append((source, target))
    return lax.ppermute(value, "ctx", pairs)


def index_of(z, y, core):
    return (z * 4 + y) * 2 + core


def other_core(z, y, core):
    return index_of(z, y, 1 - core)


def along_y(first, second):
    return lambda z, y, core: index_of(z, y ^ (second if core else first), core)


def along_z(first, second):
    return lambda z, y, core: index_of(z ^ (second if core else first), y, core)


def beside(z, y, core):
    here = index_of(z, y, core)
    there = here + 1 if core else here - 1
    return there if 0 <= there < N_CTX else None


def pooling_matrix(rows, group):
    out = lax.broadcasted_iota(jnp.int32, (rows // group, rows), 0)
    src = lax.broadcasted_iota(jnp.int32, (rows // group, rows), 1)
    return (src // group == out).astype(jnp.float32).astype(jnp.bfloat16)


def pool(value, group, matrix):
    total = jnp.dot(matrix, value, preferred_element_type=jnp.float32)
    return (total / jnp.float32(group**0.5)).astype(jnp.bfloat16)


def first_kernel(core_ref, k_hbm, v_hbm, near_ref, far_hbm, one_ref, two_ref, buf, sems, far_sem):
    core = core_ref[0]
    by4 = pooling_matrix(BLOCK, 4)
    by2 = pooling_matrix(POOL, 2)
    copies = []
    for part in range(TOK // BLOCK):
        rows = pl.ds(part * BLOCK, BLOCK)
        for side, ref in enumerate((k_hbm, v_hbm)):
            there = buf.at[rows, pl.ds(side * WIDTH, WIDTH)]
            copies.append(pltpu.make_async_copy(ref.at[rows, :], there, sems.at[2 * part + side]))
    for copy in copies:
        copy.start()
    for part in range(TOK // BLOCK):
        for side in range(2):
            copies[2 * part + side].wait()
            cols = pl.ds(side * WIDTH, WIDTH)
            zero = pool(buf[pl.ds(part * BLOCK, BLOCK), cols], 4, by4)
            near_ref[pl.ds(part * (BLOCK // 4), BLOCK // 4), cols] = zero
    first = pl.multiple_of(core * (TOK - EDGE), EDGE)
    far = pltpu.make_async_copy(buf.at[pl.ds(first, EDGE), :], far_hbm, far_sem)
    far.start()
    one = pool(near_ref[pl.ds(0, POOL), :], 2, by2)
    one_ref[...] = one
    two_ref[...] = pool(one, 2, by2[: POOL // 4, : POOL // 2])
    last = pl.multiple_of((1 - core) * (TOK - EDGE), EDGE)
    near_ref[pl.ds(POOL, EDGE), :] = buf[pl.ds(last, EDGE), :]
    far.wait()


def first_pools(core, keys, values):
    counts = (POOL + EDGE, EDGE, POOL // 2, POOL // 4)
    hbm, vmem = (pl.BlockSpec(memory_space=m) for m in (pltpu.HBM, pltpu.VMEM))
    return pl.pallas_call(
        first_kernel,
        in_specs=[pl.BlockSpec(memory_space=pltpu.SMEM), hbm, hbm],
        out_specs=[vmem, hbm, vmem, vmem],
        out_shape=[
            (pltpu.HBM if r == EDGE else pltpu.VMEM)((r, 2 * WIDTH), jnp.bfloat16) for r in counts
        ],
        scratch_shapes=[
            pltpu.VMEM((TOK, 2 * WIDTH), jnp.bfloat16),
            pltpu.SemaphoreType.DMA((2 * TOK // BLOCK,)),
            pltpu.SemaphoreType.DMA,
        ],
        compiler_params=pltpu.CompilerParams(vmem_limit_bytes=VMEM_LIMIT),
        cost_estimate=pl.CostEstimate(flops=10**8, bytes_accessed=4 * 2**20, transcendentals=0),
        name="first_pools",
    )(core, keys, values)


def small_call(kernel, rows, *operands):
    vmem = pl.BlockSpec(memory_space=pltpu.VMEM)
    return pl.pallas_call(
        kernel,
        in_specs=[vmem] * len(operands),
        out_specs=[vmem] * len(rows),
        out_shape=[jax.ShapeDtypeStruct((r, 2 * WIDTH), jnp.bfloat16) for r in rows],
        compiler_params=pltpu.CompilerParams(vmem_limit_bytes=VMEM_LIMIT),
        cost_estimate=pl.CostEstimate(flops=10**8, bytes_accessed=2**20, transcendentals=0),
    )(*operands)


def both_kernel(two_ref, near_ref, both_ref):
    both_ref[pl.ds(0, 64), :] = two_ref[...]
    by2 = pooling_matrix(POOL, 2)
    one = pool(near_ref[pl.ds(0, POOL), :], 2, by2)
    both_ref[pl.ds(64, 64), :] = pool(one, 2, by2[:64, :128])


def threes(two, one_got, twos_got, by2):
    rows = jnp.concatenate([pool(one_got, 2, by2[:64, :128]), twos_got, two], axis=0)
    return pool(rows, 2, by2)


def plane_kernel(two_ref, one_ref, twos_ref, got_ref, three_ref):
    one, twos = one_ref[...], twos_ref[...]
    got_ref[pl.ds(0, 128), :] = one
    got_ref[pl.ds(128, 128), :] = twos
    three_ref[...] = threes(two_ref[...], one, twos, pooling_matrix(256, 2))


def wide_kernel(three_ref, got_ref, both_ref, fours_ref, fives_ref):
    by2 = pooling_matrix(256, 2)
    got = got_ref[pl.ds(0, 128), :], got_ref[pl.ds(128, 128), :]
    other = threes(both_ref[pl.ds(64, 64), :], *got, by2)
    fours = pool(jnp.concatenate([three_ref[...], other], axis=0), 2, by2)
    fours_ref[...] = fours
    fives_ref[...] = pool(fours, 2, by2[:64, :128])


def times(a, b, dims):
    return lax.dot_general(a, b, (dims, ((), ())), preferred_element_type=jnp.float32)


def attend_kernel(plan, carried, final, fetched, *refs):
    refs = list(refs)
    bias = refs.pop(0)[0]
    q_ref = refs.pop(0)
    arrays = [refs.pop(0) for _ in range(1 + max(max(p[0], p[1]) for p in plan))]
    if carried:
        acc_in, m_in, l_in = refs.pop(0), refs.pop(0), refs.pop(0)
    if fetched:
        sems = refs.pop()
        held = [refs.pop(-2), refs.pop()]

        def fetch(at, h):
            lanes = pl.ds(pl.multiple_of(h * HD, HD), HD)
            there = held[at].at[:, lanes]
            return pltpu.make_async_copy(arrays[at].at[:, lanes], there, sems.at[at, h])

        for h in range(HEADS_DEV):
            for at in range(2):
                fetch(at, h).start()

    sources = held if fetched else arrays

    def lanes(first, h):
        if isinstance(h, int):
            return pl.ds(first + h * HD, HD)
        return pl.ds(pl.multiple_of(first + h * HD, HD), HD)

    def pieces_of(h):
        pieces = []
        for k_at, v_at, first, count, v_lane, masked in plan:
            rows = pl.ds(first, count)
            k, v = sources[k_at][rows, lanes(0, h)], sources[v_at][rows, lanes(v_lane, h)]
            pieces.append((k, v.T, masked))
        return pieces

    def put(h, rows, acc, peak, total):
        if final:
            refs[0][rows, lanes(0, h)] = (acc * (1.0 / total)).astype(jnp.bfloat16).T
        else:
            refs[0][h, :, rows] = acc
            refs[1][h, :, rows] = peak
            refs[2][h, :, rows] = total

    def add(v, s, peak, total, acc):
        p = jnp.exp2((s - peak) * SCALE_LOG2)
        total = total + jnp.sum(p, axis=0, keepdims=True)
        return total, acc + times(v, p.astype(jnp.bfloat16), ((1,), (0,)))

    largest = []
    for h in range(HEADS_DEV):
        if fetched:
            for at in range(2):
                fetch(at, h).wait()
        pieces = pieces_of(h)
        for first in range(0, TOK, STRIP):
            rows = pl.ds(first, STRIP)
            query = q_ref[rows, lanes(0, h)]
            acc, total = 0.0, 0.0
            if carried:
                acc, peak, total = acc_in[h, :, rows], m_in[h, :, rows], l_in[h, :, rows]
                parts = pieces
            else:
                (k, v, masked), *rest = pieces
                parts = [(k[:256], v[:, :256], masked), (k[256:], v[:, 256:], masked), *rest]
                peak = None
            for k, v, masked in parts:
                s = times(k, query, ((1,), (1,)))
                if masked:
                    s = s + bias
                if peak is None:
                    peak = jnp.max(s, axis=0, keepdims=True)
                total, acc = add(v, s, peak, total, acc)
            put(h, rows, acc, peak, total)
            largest.append(jnp.max(total, axis=1, keepdims=True))

    @pl.when(jnp.logical_not(jnp.max(functools.reduce(jnp.maximum, largest)) < TOTAL_LIMIT))
    def _():
        def one_tile(index, _):
            h = index // (TOK // Q_TILE)
            rows = pl.ds(pl.multiple_of(index % (TOK // Q_TILE) * Q_TILE, Q_TILE), Q_TILE)
            query = q_ref[rows, lanes(0, h)]
            pieces = pieces_of(h)
            scores = []
            for k, _, masked in pieces:
                s = times(k, query, ((1,), (1,)))
                scores.append(s + bias if masked else s)
            peaks = [jnp.max(s, axis=0, keepdims=True) for s in scores]
            acc, total = 0.0, 0.0
            if carried:
                before = m_in[h, :, rows]
                peaks.append(before)
            peak = functools.reduce(jnp.maximum, peaks)
            if carried:
                fade = jnp.exp2((before - peak) * SCALE_LOG2)
                acc, total = acc_in[h, :, rows] * fade, l_in[h, :, rows] * fade
            for s, (k, v, _) in zip(scores, pieces):
                total, acc = add(v, s, peak, total, acc)
            put(h, rows, acc, peak, total)
            return 0

        lax.fori_loop(0, HEADS_DEV * (TOK // Q_TILE), one_tile, 0)


def attend(bias, queries, arrays, plan, state, final, fetched=False):
    vmem = pl.BlockSpec(memory_space=pltpu.VMEM)
    operands = [bias, queries, *arrays, *state]
    count = sum(piece[3] for piece in plan)
    around, scratch = [vmem] * len(arrays), []
    if fetched:
        around = [pl.BlockSpec(memory_space=pltpu.HBM)] * len(arrays)
        scratch = [pltpu.VMEM(array.shape, array.dtype) for array in arrays]
        scratch.append(pltpu.SemaphoreType.DMA((len(arrays), HEADS_DEV)))
    if final:
        out_specs = vmem
        out_shape = jax.ShapeDtypeStruct((TOK, WIDTH), jnp.bfloat16)
    else:
        out_specs = [vmem] * 3
        out_shape = [
            jax.ShapeDtypeStruct((HEADS_DEV, rows, TOK), jnp.float32) for rows in (HD, 1, 1)
        ]
    return pl.pallas_call(
        functools.partial(attend_kernel, plan, bool(state), final, fetched),
        in_specs=[pl.BlockSpec(memory_space=pltpu.SMEM), vmem, *around, *[vmem] * len(state)],
        scratch_shapes=scratch,
        out_specs=out_specs,
        out_shape=out_shape,
        compiler_params=pltpu.CompilerParams(vmem_limit_bytes=VMEM_LIMIT),
        cost_estimate=pl.CostEstimate(
            flops=4 * TOK * count * WIDTH,
            bytes_accessed=2 * TOK * WIDTH + 4 * count * WIDTH + 4 * TOK * WIDTH,
            transcendentals=TOK * count * HEADS_DEV,
        ),
    )(*operands)


def on_device(queries, keys, values):
    position = lax.axis_index("ctx")
    core = (position % 2).astype(jnp.int32).reshape(1)
    outer = (position == 0) | (position == N_CTX - 1)
    bias = jnp.where(outer, jnp.float32(-1e30), jnp.float32(0)).reshape(1)

    keys = pltpu.with_memory_space_constraint(keys, pltpu.HBM)
    values = pltpu.with_memory_space_constraint(values, pltpu.HBM)
    near, far, one, two = first_pools(core, keys, values)
    near_got = swap(near, other_core)
    one_got = swap(one, along_y(1, 1))
    (both,) = small_call(both_kernel, (128,), two, near_got)
    twos_got = swap(both, along_y(2, 3))
    plan = ((0, 1, 0, TOK, 0, False),)
    state = attend(bias, queries, [keys, values], plan, (), False, fetched=True)
    plan = ((0, 0, 0, 512, WIDTH, False),)
    state = attend(bias, queries, [near_got], plan, state, False)
    far_got = swap(far, beside)

    planes, three = small_call(plane_kernel, (256, 128), two, one_got, twos_got)
    planes_got = swap(planes, other_core)
    three_got = swap(three, along_z(1, 1))
    fours, fives = small_call(wide_kernel, (128, 64), three, planes_got, both)
    fours_got = swap(fours, along_z(2, 3))
    fives_c = swap(fives, along_z(5, 4))
    fives_d = swap(fives, along_z(6, 7))
    plan = ((0, 0, 0, 256, WIDTH, False), (1, 1, 0, 256, WIDTH, False))
    plan += ((2, 2, 0, 256, WIDTH, True),)
    state = attend(bias, queries, [planes, planes_got, far_got], plan, state, False)

    plan = ((0, 0, 0, 256, WIDTH, False),)
    middle = jnp.concatenate([three_got, fours_got], axis=0)
    middle_got = swap(middle, other_core)
    state = attend(bias, queries, [middle], plan, state, False)
    state = attend(bias, queries, [middle_got], plan, state, False)
    plan = ((0, 0, 0, 128, WIDTH, False),)
    upper = jnp.concatenate([fives_c, fives_d], axis=0)
    upper_got = swap(upper, other_core)
    state = attend(bias, queries, [upper], plan, state, False)
    return attend(bias, queries, [upper_got], plan, state, True)


def solution(mesh):
    return jax.shard_map(
        on_device,
        mesh=mesh,
        in_specs=(P("ctx", "head"), P("ctx", "head"), P("ctx", "head")),
        out_specs=P("ctx", "head"),
        check_vma=False,
    )
```
